32 devices in a mesh: grp: 2 (over x), ka: 16 (over z, y, core).
Axes of the slice: x: 2, y: 2, z: 4, core: 2. Of those that a mesh axis runs over, the one named last changes fastest.
Arguments:
- wannier_table: float32 [2, 2048, 8192], P(None, 'grp', 'ka'), parts along dimension 1, may hold values from -0.125 to 0.125
- lattice: int32 [3, 2048], P(None, 'grp'), parts along dimension 1, may hold values from -12 to 12
- kpoint_grid: int32 [3, 2048], P(None, ('grp', 'ka')), parts along dimension 1, may hold values from 0 to 63
- eigen_vectors: float32 [2048, 64, 128], P(('grp', 'ka')), parts along dimension 0, may hold values from -0.5 to 0.5
- target_owner: int32 [2048], P(('grp', 'ka')), parts along dimension 0, may hold values from 0 to 15, as said below
- target_slot: int32 [2048], P(('grp', 'ka')), parts along dimension 0, may hold values from 0 to 63
Outputs:
- rotated_coupling: float32 [2048, 2, 64, 128], P(('grp', 'ka')), parts along dimension 0
The draws below stay inside these ranges and needn't reach their ends.
There are 2 independent parts, one for each index of `grp`. The reference program is written for one: setup_inputs(seed, part) draws one part's arguments, and reference() takes and returns one part's arrays. A program takes and returns all parts, laid end to end along the dimension named above; each array names one. Nothing has to cross between parts.
Inputs may be any that keep to these rules, and one draw needn't show every extreme that they name: target_owner[k] * 64 + target_slot[k] over all k is a permutation of the 1024 k-points. The 64 k-points of one index of ka ask at most 8 of them of any one owner, and every device asks exactly 8 of some owner.
All inputs are finite; a program needn't handle non-finite values.
Results may differ from the reference program's by a relative error of at most 0.0003.
Values sent between devices are 32-bit elements; how exact they have to be, the bound alone decides.
No kernel may reach another device: no remote copies, remote signals or barrier semaphores. Data moves between devices by JAX's collectives and lax.ppermute only.
A program may use at most 128 MiB of HBM per device.

```python
import math
import jax
import jax.numpy as jnp
from jax import lax

NW = 64
NMODE = 2
NRVEC = 1024
KMESH = 64
K_DEV = 64
KPTS = 1024
PAIRS = 8192
N_KA = 16


def target_pairs(key):
    base = jax.random.fold_in(key, 17)
    key_pairing, key_excess, key_offsets, key_slots, key_order = jax.random.split(base, 5)
    per_owner = K_DEV // N_KA
    halves = N_KA // 2
    pairing = jax.random.permutation(key_pairing, N_KA)
    excess = jax.random.randint(key_excess, (halves,), 0, per_owner + 1).astype(jnp.int32).at[0].set(per_owner)
    multiplicity = jnp.zeros((N_KA,), jnp.int32).at[pairing[:halves]].set(per_owner + excess).at[pairing[halves:]].set(per_owner - excess)
    offsets = jnp.repeat(jnp.arange(N_KA, dtype=jnp.int32), multiplicity, total_repeat_length=K_DEV)
    offsets = jax.random.permutation(key_offsets, offsets)
    slots = jax.random.permutation(key_slots, K_DEV).astype(jnp.int32)
    shuffles = jax.vmap(lambda subkey: jax.random.permutation(subkey, K_DEV))(jax.random.split(key_order, N_KA))
    device_ids = jnp.arange(N_KA, dtype=jnp.int32)[:, None]
    owners = (device_ids + offsets[shuffles]) % N_KA
    local_slots = slots[shuffles]
    return (owners.reshape(-1).astype(jnp.int32), local_slots.reshape(-1).astype(jnp.int32))


def draw_target_owner(key, part):
    return target_pairs(key)[0]


def draw_target_slot(key, part):
    return target_pairs(key)[1]


def with_ends(drawn, key, smallest, high):
    shape = drawn.shape
    spot = [jax.random.randint(jax.random.fold_in(key, axis), (), 0, shape[axis]) for axis in range(len(shape))]
    drawn = drawn.at[tuple(spot)].set(smallest)
    longest = shape.index(max(shape))
    spot[longest] = (spot[longest] + 1) % shape[longest]
    return drawn.at[tuple(spot)].set(high)


def levels(rng, shape, shards, low, top_value):
    level = 1.0
    for axis_at, shards_of in shards:
        steps = jax.random.uniform(jax.random.fold_in(jax.random.fold_in(rng, 6), axis_at), (shards_of,), jnp.float32, low / len(shards), top_value / len(shards))
        level = level * jnp.repeat(jnp.exp(steps), shape[axis_at] // shards_of).reshape((-1,) + (1,) * (len(shape) - 1 - axis_at))
    return level


def scatter_about(key, extent, scale, most, cuts=(), kind=jnp.bfloat16):
    values = jax.random.normal(key, extent, jnp.float32) * scale
    if len(cuts) > 0:
        values = levels(key, extent, cuts, -0.22, 0.18) * values
    return jnp.clip(values, min=-most, max=most).astype(kind)


def setup_inputs(seed: int = 0, part: int = 0) -> dict:
    splits = jax.random.split(jax.random.key(seed), 7)
    own_keys = jax.random.split(jax.random.fold_in(splits[6], part), 7)
    wannier_table = scatter_about(own_keys[0], (2, NRVEC, PAIRS), (2 * NRVEC) ** -0.5, 0.125, ((2, 16),), jnp.float32)
    lattice = with_ends(jax.random.randint(own_keys[1], (3, NRVEC), -12, 13), jax.random.fold_in(own_keys[1], 1), -12, 12).astype(jnp.int32)
    kpoint_grid = with_ends(jax.random.randint(own_keys[2], (3, KPTS), 0, KMESH), jax.random.fold_in(own_keys[2], 1), 0, KMESH - 1).astype(jnp.int32)
    eigen_vectors = scatter_about(own_keys[3], (KPTS, NW, 2 * NW), (2 * NW) ** -0.5, 0.5, ((0, 16),), jnp.float32)
    target_owner = draw_target_owner(jax.random.fold_in(jax.random.fold_in(splits[6], part), 71), part)
    target_slot = draw_target_slot(jax.random.fold_in(jax.random.fold_in(splits[6], part), 71), part)
    return {"wannier_table": wannier_table, "lattice": lattice, "kpoint_grid": kpoint_grid, "eigen_vectors": eigen_vectors, "target_owner": target_owner, "target_slot": target_slot}


def phases(grid_block, lattice):
    products = grid_block[0][:, None] * lattice[0][None, :] + grid_block[1][:, None] * lattice[1][None, :] + grid_block[2][:, None] * lattice[2][None, :]
    angles = jnp.mod(products, KMESH).astype(jnp.float32) * (2.0 * math.pi / KMESH)
    return jnp.cos(angles), jnp.sin(angles)


def rotate(real_part, imag_part, near_vectors, far_vectors):
    orbitals = near_vectors.shape[1]
    highest = lax.Precision.HIGHEST
    near_swap = jnp.concatenate([-near_vectors[..., orbitals:], near_vectors[..., :orbitals]], -1)
    right_done = jnp.einsum("kamn,knj->kamj", real_part, near_vectors, precision=highest) + jnp.einsum("kamn,knj->kamj", imag_part, near_swap, precision=highest)
    right_swap = jnp.concatenate([right_done[..., orbitals:], -right_done[..., :orbitals]], -1)
    return jnp.einsum("kmi,kamj->kaij", far_vectors[..., :orbitals], right_done, precision=highest) + jnp.einsum("kmi,kamj->kaij", far_vectors[..., orbitals:], right_swap, precision=highest)


def reference(wannier_table, lattice, kpoint_grid, eigen_vectors, target_owner, target_slot):
    block_rows = math.gcd(KPTS, 512)
    highest = lax.Precision.HIGHEST
    target = (target_owner * K_DEV + target_slot).astype(jnp.int32)

    def one_block(block_id):
        first = (block_id * block_rows).astype(jnp.int32)
        grid_block = lax.dynamic_slice_in_dim(kpoint_grid, first, block_rows, 1)
        cosine, sine_part = phases(grid_block, lattice)
        real_part = jnp.dot(cosine, wannier_table[0], precision=highest) - jnp.dot(sine_part, wannier_table[1], precision=highest)
        imag_part = jnp.dot(cosine, wannier_table[1], precision=highest) + jnp.dot(sine_part, wannier_table[0], precision=highest)
        real_part = real_part.reshape(block_rows, NMODE, NW, NW)
        imag_part = imag_part.reshape(block_rows, NMODE, NW, NW)
        near_vectors = lax.dynamic_slice_in_dim(eigen_vectors, first, block_rows, 0)
        far_vectors = eigen_vectors[lax.dynamic_slice_in_dim(target, first, block_rows, 0)]
        return rotate(real_part, imag_part, near_vectors, far_vectors)

    blocks = lax.map(one_block, jnp.arange(KPTS // block_rows, dtype=jnp.int32))
    return blocks.reshape(KPTS, NMODE, NW, 2 * NW)
```

```python
import math

import jax
import jax.numpy as jnp
from jax import lax
from jax.experimental import pallas as pl
from jax.experimental.pallas import tpu as pltpu
from jax.sharding import PartitionSpec as P

KMESH = 64
CHUNKS = 4

SIN_TERMS = [(-1.0) ** i * math.pi ** (2 * i + 1) / math.factorial(2 * i + 1) for i in range(7)]
COS_TERMS = [(-1.0) ** i * math.pi ** (2 * i) / math.factorial(2 * i) for i in range(8)]


def horner(terms, x):
    total = jnp.full_like(x, terms[-1])
    for term in terms[-2::-1]:
        total = total * x + term
    return total


def split(x):
    high = x.astype(jnp.bfloat16)
    return high, (x - high.astype(jnp.float32)).astype(jnp.bfloat16)


def dot(a, b):
    return jnp.dot(a, b, preferred_element_type=jnp.float32)


def dot3(a, b):
    return dot(a[0], b[0]) + dot(a[0], b[1]) + dot(a[1], b[0])


def table_kernel(table, high, low):
    half = pl.program_id(0)
    pairs = table.shape[2]
    lane = lax.broadcasted_iota(jnp.int32, (table.shape[1], 128), 1)
    first = lane < 64
    for block in range(pairs // 128):
        cut = slice(block * 128, (block + 1) * 128)

        def put(at, value):
            a, b = split(value)
            high[:, at * 128 : (at + 1) * 128] = a
            low[:, at * 128 : (at + 1) * 128] = b

        @pl.when(half == 0)
        def _():
            real, imag = table[0, :, cut], table[1, :, cut]
            put(2 * block, jnp.where(first, real, pltpu.roll(imag, 64, 1)))
            put(2 * block + 1, jnp.where(first, pltpu.roll(real, 64, 1), imag))

        @pl.when(half == 1)
        def _():
            real, imag = table[0, :, cut], table[1, :, cut]
            put(2 * block, jnp.where(first, -imag, pltpu.roll(real, 64, 1)))
            put(2 * block + 1, jnp.where(first, -pltpu.roll(imag, 64, 1), real))


def prepare_table(table):
    vectors, pairs = table.shape[1:]
    rows = min(vectors, 256)
    steps = vectors // rows
    return pl.pallas_call(
        table_kernel,
        out_shape=[jax.ShapeDtypeStruct((2 * vectors, 2 * pairs), jnp.bfloat16)] * 2,
        grid=(2, steps),
        in_specs=[pl.BlockSpec((2, rows, pairs), lambda h, i: (0, i, 0))],
        out_specs=[pl.BlockSpec((rows, 2 * pairs), lambda h, i: (h * steps + i, 0))] * 2,
        name="table",
    )(table)


def interpolate_kernel(grid_rows, lattice, high, low, out, *, mrows):
    turns = dot(grid_rows[...].astype(jnp.bfloat16), lattice[...].astype(jnp.bfloat16)) * (1.0 / KMESH)
    part = turns - jnp.round(turns)
    square = part * part
    sine = horner(SIN_TERMS, square) * part
    cosine = horner(COS_TERMS, square)
    phase = jnp.concatenate([1.0 - 2.0 * sine * sine, 2.0 * sine * cosine], 1)
    result = dot3(split(phase), (high[...], low[...]))
    rows = result.shape[0]
    for m in range(mrows):
        out[pl.ds(m, rows, stride=mrows), :] = result[:, m * 128 : (m + 1) * 128]


def interpolate(grid_rows, lattice, high, low, mrows):
    rows = grid_rows.shape[0]
    step = min(rows, 256)
    whole = lambda a: pl.BlockSpec(a.shape, lambda i: (0, 0))
    return pl.pallas_call(
        lambda *refs: interpolate_kernel(*refs, mrows=mrows),
        out_shape=jax.ShapeDtypeStruct((rows * mrows, 128), jnp.float32),
        grid=(rows // step,),
        in_specs=[
            pl.BlockSpec((step, grid_rows.shape[1]), lambda i: (i, 0)),
            whole(lattice),
            whole(high),
            whole(low),
        ],
        out_specs=pl.BlockSpec((step * mrows, 128), lambda i: (i, 0)),
        name="interpolate",
    )(grid_rows, lattice, high, low)


def rotate_kernel(coupling, near, far, out, *, block, mrows):
    first = lax.broadcasted_iota(jnp.int32, (64, 128), 1) < 64
    first2 = lax.broadcasted_iota(jnp.int32, (128, 128), 1) < 64
    for k in range(block):
        if mrows:
            values = coupling[:, k * mrows : (k + 1) * mrows, :].reshape(128, 128)
        else:
            values = coupling[k]
        u = near[k]
        u_turned = pltpu.roll(u, 64, 1)
        u_full = jnp.concatenate([u, jnp.where(first, -u_turned, u_turned)], 0)
        right = dot3(split(values), split(u_full))
        turned = pltpu.roll(right, 64, 1)
        turned = jnp.where(first2, turned, -turned)
        v = far[k].T
        left = jnp.concatenate([v[:64], v[64:]], 1)
        stacked = jnp.concatenate(
            [
                jnp.concatenate([right[:64], right[64:]], 1),
                jnp.concatenate([turned[:64], turned[64:]], 1),
            ],
            0,
        )
        done = dot3(split(left), split(stacked))
        out[k, 0] = done[:, :128]
        out[k, 1] = done[:, 128:]


def rotate(coupling, near, far, mrows):
    kpoints, orbitals = near.shape[:2]
    block = min(kpoints, 8)
    if mrows % 8:
        sources = coupling.shape[0]
        coupling = (
            coupling.reshape(sources, kpoints, mrows, 128)
            .transpose(1, 0, 2, 3)
            .reshape(kpoints, sources * mrows, 128)
        )
        mrows = 0
        coupling_spec = pl.BlockSpec((block,) + coupling.shape[1:], lambda i: (i, 0, 0))
    else:
        coupling_spec = pl.BlockSpec((coupling.shape[0], block * mrows, 128), lambda i: (0, i, 0))
    vector_spec = pl.BlockSpec((block, orbitals, 2 * orbitals), lambda i: (i, 0, 0))
    return pl.pallas_call(
        lambda *refs: rotate_kernel(*refs, block=block, mrows=mrows),
        out_shape=jax.ShapeDtypeStruct((kpoints, 2, orbitals, 2 * orbitals), jnp.float32),
        grid=(kpoints // block,),
        in_specs=[coupling_spec, vector_spec, vector_spec],
        out_specs=pl.BlockSpec((block, 2, orbitals, 2 * orbitals), lambda i: (i, 0, 0, 0)),
        name="rotate",
    )(coupling, near, far)


def exchange(x):
    return lax.all_to_all(x, "ka", split_axis=0, concat_axis=0, tiled=True)


def local(wannier_table, lattice, kpoint_grid, eigen_vectors, target_owner, target_slot):
    kpoints, orbitals = eigen_vectors.shape[:2]
    vectors, pairs = wannier_table.shape[1:]
    devices = lax.axis_size("ka")
    me = lax.axis_index("ka")
    mrows = pairs // orbitals
    capacity = 2 * kpoints // devices

    own = jnp.concatenate(
        [kpoint_grid, target_owner[None], target_slot[None], jnp.zeros((3, kpoints), jnp.int32)], 0
    )
    known = exchange(jnp.broadcast_to(own[None], (devices, 8, kpoints)))
    high, low = prepare_table(wannier_table)

    asked = known[:, 3] == me
    position = jnp.cumsum(asked.astype(jnp.int32), 1) - 1
    chosen = asked[:, None, :] & (position[:, None, :] == jnp.arange(capacity)[None, :, None])
    wanted = jnp.sum(jnp.where(chosen, known[:, 4][:, None, :], 0), 2)
    picked = eigen_vectors[wanted.reshape(-1)].reshape(devices, capacity * orbitals, 2 * orbitals)
    fetched = exchange(picked).reshape(devices * capacity, orbitals, 2 * orbitals)

    owners = (target_owner[:, None] == jnp.arange(devices, dtype=jnp.int32)[None, :]).astype(jnp.int32)
    before = jnp.cumsum(owners, 0) - owners
    flat_index = target_owner * capacity + jnp.sum(before * owners, 1)

    grid_rows = known.transpose(0, 2, 1).astype(jnp.float32)
    lattice_rows = jnp.concatenate([lattice, jnp.zeros((5, vectors), jnp.int32)], 0).astype(jnp.float32)
    per_chunk = kpoints // CHUNKS
    sent = []
    for c in range(CHUNKS):
        rows = grid_rows[:, c * per_chunk : (c + 1) * per_chunk].reshape(devices * per_chunk, 8)
        values = interpolate(rows, lattice_rows, high, low, mrows)
        sent.append(exchange(values.reshape(devices, per_chunk * mrows, 128)))
    far = fetched[flat_index]
    done = []
    for c in range(CHUNKS):
        cut = slice(c * per_chunk, (c + 1) * per_chunk)
        done.append(rotate(sent[c], eigen_vectors[cut], far[cut], mrows))
    return jnp.concatenate(done, 0)


def solution(mesh):
    placed = (
        P(None, "grp", "ka"),
        P(None, "grp"),
        P(None, ("grp", "ka")),
        P(("grp", "ka"), None, None),
        P(("grp", "ka")),
        P(("grp", "ka")),
    )
    return jax.shard_map(
        local,
        mesh=mesh,
        in_specs=placed,
        out_specs=P(("grp", "ka"), None, None, None),
        check_vma=False,
    )
```

```python
import math

import jax
import jax.numpy as jnp
from jax import lax
from jax.experimental import pallas as pl
from jax.experimental.pallas import tpu as pltpu
from jax.sharding import PartitionSpec as P

KMESH = 64

SIN_TERMS = [(-1.0) ** i * math.pi ** (2 * i + 1) / math.factorial(2 * i + 1) for i in range(7)]
COS_TERMS = [(-1.0) ** i * math.pi ** (2 * i) / math.factorial(2 * i) for i in range(8)]


def horner(terms, x):
    total = jnp.full_like(x, terms[-1])
    for term in terms[-2::-1]:
        total = total * x + term
    return total


def split(x):
    high = x.astype(jnp.bfloat16)
    return high, (x - high.astype(jnp.float32)).astype(jnp.bfloat16)


def dot(a, b):
    return jnp.dot(a, b, preferred_element_type=jnp.float32)


def dot3(a, b):
    return dot(a[0], b[0]) + dot(a[0], b[1]) + dot(a[1], b[0])


def table_kernel(table, high, low):
    half = pl.program_id(0)
    pairs = table.shape[2]
    lane = lax.broadcasted_iota(jnp.int32, (table.shape[1], 128), 1)
    first = lane < 64
    for block in range(pairs // 128):
        cut = slice(block * 128, (block + 1) * 128)

        def put(at, value):
            a, b = split(value)
            high[:, at * 128 : (at + 1) * 128] = a
            low[:, at * 128 : (at + 1) * 128] = b

        @pl.when(half == 0)
        def _():
            real, imag = table[0, :, cut], table[1, :, cut]
            put(2 * block, jnp.where(first, real, pltpu.roll(imag, 64, 1)))
            put(2 * block + 1, jnp.where(first, pltpu.roll(real, 64, 1), imag))

        @pl.when(half == 1)
        def _():
            real, imag = table[0, :, cut], table[1, :, cut]
            put(2 * block, jnp.where(first, -imag, pltpu.roll(real, 64, 1)))
            put(2 * block + 1, jnp.where(first, -pltpu.roll(imag, 64, 1), real))


def prepare_table(table):
    vectors, pairs = table.shape[1:]
    rows = min(vectors, 256)
    steps = vectors // rows
    return pl.pallas_call(
        table_kernel,
        out_shape=[jax.ShapeDtypeStruct((2 * vectors, 2 * pairs), jnp.bfloat16)] * 2,
        grid=(2, steps),
        in_specs=[pl.BlockSpec((2, rows, pairs), lambda h, i: (0, i, 0))],
        out_specs=[pl.BlockSpec((rows, 2 * pairs), lambda h, i: (h * steps + i, 0))] * 2,
        name="table",
    )(table)


def interpolate_kernel(grid_rows, lattice, high, low, out, *, mrows):
    turns = dot(grid_rows[...].astype(jnp.bfloat16), lattice[...].astype(jnp.bfloat16)) * (1.0 / KMESH)
    part = turns - jnp.round(turns)
    square = part * part
    sine = horner(SIN_TERMS, square) * part
    cosine = horner(COS_TERMS, square)
    phase = jnp.concatenate([1.0 - 2.0 * sine * sine, 2.0 * sine * cosine], 1)
    result = dot3(split(phase), (high[...], low[...]))
    rows = result.shape[0]
    for m in range(mrows):
        out[pl.ds(m, rows, stride=mrows), :] = result[:, m * 128 : (m + 1) * 128]


def interpolate(grid_rows, lattice, high, low, mrows):
    rows = grid_rows.shape[0]
    step = min(rows, 256)
    whole = lambda a: pl.BlockSpec(a.shape, lambda i: (0, 0))
    return pl.pallas_call(
        lambda *refs: interpolate_kernel(*refs, mrows=mrows),
        out_shape=jax.ShapeDtypeStruct((rows * mrows, 128), jnp.float32),
        grid=(rows // step,),
        in_specs=[
            pl.BlockSpec((step, grid_rows.shape[1]), lambda i: (i, 0)),
            whole(lattice),
            whole(high),
            whole(low),
        ],
        out_specs=pl.BlockSpec((step * mrows, 128), lambda i: (i, 0)),
        name="interpolate",
    )(grid_rows, lattice, high, low)


def rotate_one(values, u, far, orbitals):
    lanes = 2 * orbitals
    first = lax.broadcasted_iota(jnp.int32, (orbitals, lanes), 1) < orbitals
    first_all = lax.broadcasted_iota(jnp.int32, (values.shape[0], lanes), 1) < orbitals
    u_turned = pltpu.roll(u, orbitals, 1)
    u_full = jnp.concatenate([u, jnp.where(first, -u_turned, u_turned)], 0)
    right = dot3(split(values), split(u_full))
    turned = pltpu.roll(right, orbitals, 1)
    turned = jnp.where(first_all, turned, -turned)
    v = far.T
    left = jnp.concatenate([v[:orbitals], v[orbitals:]], 1)
    modes = values.shape[0] // orbitals
    by_mode = lambda x: jnp.concatenate([x[a * orbitals : (a + 1) * orbitals] for a in range(modes)], 1)
    done = dot3(split(left), split(jnp.concatenate([by_mode(right), by_mode(turned)], 0)))
    return [done[:, a * lanes : (a + 1) * lanes] for a in range(modes)]


def rotate_kernel(place, *refs, block, mrows, parts, orbitals):
    pieces = refs[:parts]
    near, far = refs[parts : parts + 2]
    out, gathered = refs[-2:]
    for k in range(block):
        if mrows:
            for s in range(parts):
                at = pl.multiple_of(lax.rem(place[0] + (parts - s), parts) * mrows, mrows)
                gathered[k, pl.ds(at, mrows), :] = pieces[s][k * mrows : (k + 1) * mrows, :]
            values = gathered[k]
        else:
            values = pieces[0][k]
        for a, done in enumerate(rotate_one(values, near[k], far[k], orbitals)):
            out[k, a] = done


def rotate(pieces, near, far, mrows, modes, start, place, before):
    total, orbitals = near.shape[:2]
    kpoints = far.shape[0]
    block = math.gcd(kpoints, 8)
    first = start // block
    lanes = 2 * orbitals
    if mrows:
        piece_spec = pl.BlockSpec((block * mrows, lanes), lambda i, _: (i, 0))
    else:
        piece_spec = pl.BlockSpec((block, modes * orbitals, lanes), lambda i, _: (i, 0, 0))
    prior = [] if before is None else [before]
    return pl.pallas_call(
        lambda *refs: rotate_kernel(
            *refs, block=block, mrows=mrows, parts=len(pieces), orbitals=orbitals
        ),
        out_shape=jax.ShapeDtypeStruct((total, modes, orbitals, lanes), jnp.float32),
        grid_spec=pltpu.PrefetchScalarGridSpec(
            num_scalar_prefetch=1,
            grid=(kpoints // block,),
            in_specs=[piece_spec] * len(pieces)
            + [
                pl.BlockSpec((block, orbitals, lanes), lambda i, _: (first + i, 0, 0)),
                pl.BlockSpec((block, orbitals, lanes), lambda i, _: (i, 0, 0)),
            ]
            + [pl.BlockSpec(memory_space=pl.ANY)] * len(prior),
            out_specs=pl.BlockSpec((block, modes, orbitals, lanes), lambda i, _: (first + i, 0, 0, 0)),
            scratch_shapes=[pltpu.VMEM((block, modes * orbitals, lanes), jnp.float32)],
        ),
        input_output_aliases={len(pieces) + 3: 0} if prior else {},
        name="rotate",
    )(place, *pieces, near, far, *prior)


def exchange(x):
    return lax.all_to_all(x, "ka", split_axis=0, concat_axis=0, tiled=True)


def shift_order(devices):
    far_first = sorted(range(1, devices), key=lambda s: -min(s, devices - s))
    order = []
    while far_first:
        order.append(far_first.pop(0))
        if far_first:
            order.append(far_first.pop())
    return order


def spread(blocks, devices):
    got = {0: blocks(0)}
    for s in shift_order(devices):
        got[s] = lax.ppermute(blocks(s), "ka", [(d, (d + s) % devices) for d in range(devices)])
    return [got[s] for s in range(devices)]


def local(wannier_table, lattice, kpoint_grid, eigen_vectors, target_owner, target_slot):
    kpoints, orbitals = eigen_vectors.shape[:2]
    vectors, pairs = wannier_table.shape[1:]
    devices = lax.axis_size("ka")
    me = lax.axis_index("ka")
    mrows = pairs // orbitals
    modes = devices * mrows // orbitals
    lanes = 2 * orbitals
    capacity = 2 * kpoints // devices
    by_shift = devices <= 16 and mrows % 8 == 0

    own = jnp.concatenate(
        [kpoint_grid, target_owner[None], target_slot[None], jnp.zeros((3, kpoints), jnp.int32)], 0
    )
    known = exchange(jnp.broadcast_to(own[None], (devices, 8, kpoints)))
    if by_shift:
        known = lax.dynamic_slice_in_dim(jnp.concatenate([known, known], 0), me, devices, 0)
    high, low = prepare_table(wannier_table)

    asked = known[:, 3] == me
    position = jnp.cumsum(asked.astype(jnp.int32), 1) - 1
    chosen = asked[:, None, :] & (position[:, None, :] == jnp.arange(capacity)[None, :, None])
    wanted = jnp.sum(jnp.where(chosen, known[:, 4][:, None, :], 0), 2)
    if by_shift:
        fetched = jnp.concatenate(spread(lambda s: eigen_vectors[wanted[s]], devices), 0)
        place_of = lax.rem(me + devices - target_owner, devices)
    else:
        picked = eigen_vectors[wanted.reshape(-1)].reshape(devices, capacity * orbitals, lanes)
        fetched = exchange(picked).reshape(devices * capacity, orbitals, lanes)
        place_of = target_owner

    owners = (target_owner[:, None] == jnp.arange(devices, dtype=jnp.int32)[None, :]).astype(jnp.int32)
    before = jnp.cumsum(owners, 0) - owners
    far = fetched[place_of * capacity + jnp.sum(before * owners, 1)]

    grid_rows = known.transpose(0, 2, 1).astype(jnp.float32)
    lattice_rows = jnp.concatenate([lattice, jnp.zeros((5, vectors), jnp.int32)], 0).astype(jnp.float32)
    cuts = [(0, kpoints // 4 * 3), (kpoints // 4 * 3, kpoints)]
    sent = []
    for start, end in cuts:
        rows = grid_rows[:, start:end].reshape(devices * (end - start), 8)
        values = interpolate(rows, lattice_rows, high, low, mrows)
        values = values.reshape(devices, (end - start) * mrows, lanes)
        if by_shift:
            sent.append(spread(lambda s: values[s], devices))
        else:
            values = exchange(values).reshape(devices, end - start, mrows, lanes)
            sent.append([values.transpose(1, 0, 2, 3).reshape(end - start, devices * mrows, lanes)])
    out = None
    place = me.astype(jnp.int32).reshape(1)
    for (start, end), pieces in zip(cuts, sent):
        out = rotate(
            pieces, eigen_vectors, far[start:end], mrows if by_shift else 0, modes, start, place, out
        )
    return out


def solution(mesh):
    placed = (
        P(None, "grp", "ka"),
        P(None, "grp"),
        P(None, ("grp", "ka")),
        P(("grp", "ka"), None, None),
        P(("grp", "ka")),
        P(("grp", "ka")),
    )
    return jax.shard_map(
        local,
        mesh=mesh,
        in_specs=placed,
        out_specs=P(("grp", "ka"), None, None, None),
        check_vma=False,
    )
```

```python
import math

import jax
import jax.numpy as jnp
from jax import lax
from jax.experimental import pallas as pl
from jax.experimental.pallas import tpu as pltpu
from jax.sharding import PartitionSpec as P


KMESH = 64
SHIFTED = 16

SIN_TERMS = [(-1.0) ** i * math.pi ** (2 * i + 1) / math.factorial(2 * i + 1) for i in range(7)]
COS_TERMS = [(-1.0) ** i * math.pi ** (2 * i) / math.factorial(2 * i) for i in range(8)]


def horner(terms, x):
    total = jnp.full_like(x, terms[-1])
    for term in terms[-2::-1]:
        total = total * x + term
    return total


def split(x):
    high = x.astype(jnp.bfloat16)
    return high, (x - high.astype(jnp.float32)).astype(jnp.bfloat16)


def dot(a, b):
    return jnp.dot(a, b, preferred_element_type=jnp.float32)


def dot3(a, b):
    return dot(a[0], b[0]) + dot(a[0], b[1]) + dot(a[1], b[0])


def table_kernel(table, high, low):
    half = pl.program_id(0)
    pairs = table.shape[2]
    lane = lax.broadcasted_iota(jnp.int32, (table.shape[1], 128), 1)
    first = lane < 64
    for block in range(pairs // 128):
        cut = slice(block * 128, (block + 1) * 128)

        def put(at, value):
            a, b = split(value)
            high[:, at * 128 : (at + 1) * 128] = a
            low[:, at * 128 : (at + 1) * 128] = b

        @pl.when(half == 0)
        def _():
            real, imag = table[0, :, cut], table[1, :, cut]
            put(2 * block, jnp.where(first, real, pltpu.roll(imag, 64, 1)))
            put(2 * block + 1, jnp.where(first, pltpu.roll(real, 64, 1), imag))

        @pl.when(half == 1)
        def _():
            real, imag = table[0, :, cut], table[1, :, cut]
            put(2 * block, jnp.where(first, -imag, pltpu.roll(real, 64, 1)))
            put(2 * block + 1, jnp.where(first, -pltpu.roll(imag, 64, 1), real))


def prepare_table(table):
    vectors, pairs = table.shape[1:]
    rows = min(vectors, 256)
    steps = vectors // rows
    return pl.pallas_call(
        table_kernel,
        out_shape=[jax.ShapeDtypeStruct((2 * vectors, 2 * pairs), jnp.bfloat16)] * 2,
        grid=(2, steps),
        in_specs=[pl.BlockSpec((2, rows, pairs), lambda h, i: (0, i, 0))],
        out_specs=[pl.BlockSpec((rows, 2 * pairs), lambda h, i: (h * steps + i, 0))] * 2,
        name="table",
    )(table)


def interpolate_kernel(grid_rows, lattice, high, low, out, *, mrows):
    turns = dot(grid_rows[...].astype(jnp.bfloat16), lattice[...].astype(jnp.bfloat16)) * (1.0 / KMESH)
    part = turns - jnp.round(turns)
    square = part * part
    sine = horner(SIN_TERMS, square) * part
    cosine = horner(COS_TERMS, square)
    phase = jnp.concatenate([1.0 - 2.0 * sine * sine, 2.0 * sine * cosine], 1)
    result = dot3(split(phase), (high[...], low[...]))
    rows = result.shape[0]
    for m in range(mrows):
        out[pl.ds(m, rows, stride=mrows), :] = result[:, m * 128 : (m + 1) * 128]


def interpolate(grid_rows, lattice, high, low, mrows):
    rows = grid_rows.shape[0]
    step = min(rows, 256)
    whole = lambda a: pl.BlockSpec(a.shape, lambda i: (0, 0))
    return pl.pallas_call(
        lambda *refs: interpolate_kernel(*refs, mrows=mrows),
        out_shape=jax.ShapeDtypeStruct((rows * mrows, 128), jnp.float32),
        grid=(rows // step,),
        in_specs=[
            pl.BlockSpec((step, grid_rows.shape[1]), lambda i: (i, 0)),
            whole(lattice),
            whole(high),
            whole(low),
        ],
        out_specs=pl.BlockSpec((step * mrows, 128), lambda i: (i, 0)),
        name="interpolate",
    )(grid_rows, lattice, high, low)


def rotate_one(values, u, far, orbitals):
    lanes = 2 * orbitals
    first = lax.broadcasted_iota(jnp.int32, (orbitals, lanes), 1) < orbitals
    first_all = lax.broadcasted_iota(jnp.int32, (values.shape[0], lanes), 1) < orbitals
    u_turned = pltpu.roll(u, orbitals, 1)
    u_full = jnp.concatenate([u, jnp.where(first, -u_turned, u_turned)], 0)
    right = dot3(split(values), split(u_full))
    turned = pltpu.roll(right, orbitals, 1)
    turned = jnp.where(first_all, turned, -turned)
    v = far.T
    left = jnp.concatenate([v[:orbitals], v[orbitals:]], 1)
    modes = values.shape[0] // orbitals
    by_mode = lambda x: jnp.concatenate([x[a * orbitals : (a + 1) * orbitals] for a in range(modes)], 1)
    done = dot3(split(left), split(jnp.concatenate([by_mode(right), by_mode(turned)], 0)))
    return [done[:, a * lanes : (a + 1) * lanes] for a in range(modes)]


def rotate_kernel(place, *refs, block, mrows, parts, orbitals):
    pieces = refs[:parts]
    near, far = refs[parts : parts + 2]
    out, gathered = refs[-2:]
    for k in range(block):
        if parts == 1 and mrows:
            values = pieces[0][:, k * mrows : (k + 1) * mrows, :].reshape(gathered.shape[1:])
        elif mrows:
            for s in range(parts):
                at = pl.multiple_of(lax.rem(place[0] + (parts - s), parts) * mrows, mrows)
                gathered[k, pl.ds(at, mrows), :] = pieces[s][k * mrows : (k + 1) * mrows, :]
            values = gathered[k]
        else:
            values = pieces[0][k]
        for a, done in enumerate(rotate_one(values, near[k], far[k], orbitals)):
            out[k, a] = done


def rotate(pieces, near, far, mrows, modes, start, place, before):
    total, orbitals = near.shape[:2]
    block = 8
    first = start // block
    lanes = 2 * orbitals
    if mrows and len(pieces) == 1:
        kpoints = pieces[0].shape[1] // mrows
        piece_spec = pl.BlockSpec((pieces[0].shape[0], block * mrows, lanes), lambda i, _: (0, i, 0))
    elif mrows:
        kpoints = pieces[0].shape[0] // mrows
        piece_spec = pl.BlockSpec((block * mrows, lanes), lambda i, _: (i, 0))
    else:
        kpoints = pieces[0].shape[0]
        piece_spec = pl.BlockSpec((block, modes * orbitals, lanes), lambda i, _: (i, 0, 0))
    prior = [] if before is None else [before]
    return pl.pallas_call(
        lambda *refs: rotate_kernel(
            *refs, block=block, mrows=mrows, parts=len(pieces), orbitals=orbitals
        ),
        out_shape=jax.ShapeDtypeStruct((total, modes, orbitals, lanes), jnp.float32),
        grid_spec=pltpu.PrefetchScalarGridSpec(
            num_scalar_prefetch=1,
            grid=(kpoints // block,),
            in_specs=[piece_spec] * len(pieces)
            + [
                pl.BlockSpec((block, orbitals, lanes), lambda i, _: (first + i, 0, 0)),
                pl.BlockSpec((block, orbitals, lanes), lambda i, _: (first + i, 0, 0)),
            ]
            + [pl.BlockSpec(memory_space=pl.ANY)] * len(prior),
            out_specs=pl.BlockSpec((block, modes, orbitals, lanes), lambda i, _: (first + i, 0, 0, 0)),
            scratch_shapes=[pltpu.VMEM((block, modes * orbitals, lanes), jnp.float32)],
        ),
        input_output_aliases={len(pieces) + 3: 0} if prior else {},
        name="rotate",
    )(place, *pieces, near, far, *prior)


def exchange(x):
    return lax.all_to_all(x, "ka", split_axis=0, concat_axis=0, tiled=True)


def shift_order(devices):
    far_first = sorted(range(1, devices), key=lambda s: -min(s, devices - s))
    order = []
    while far_first:
        order.append(far_first.pop(0))
        if far_first:
            order.append(far_first.pop())
    return order


def spread(blocks, devices):
    got = {0: blocks(0)}
    for s in shift_order(devices):
        got[s] = lax.ppermute(blocks(s), "ka", [(d, (d + s) % devices) for d in range(devices)])
    return [got[s] for s in range(devices)]


def placed_local(wannier_table, lattice, kpoint_grid, eigen_vectors, target_owner, target_slot):
    kpoints, orbitals = eigen_vectors.shape[:2]
    vectors, pairs = wannier_table.shape[1:]
    devices = lax.axis_size("ka")
    me = lax.axis_index("ka")
    mrows = pairs // orbitals
    modes = devices * mrows // orbitals
    lanes = 2 * orbitals
    capacity = 2 * kpoints // devices
    tiled = mrows % 8 == 0
    by_shift = devices <= SHIFTED and tiled

    own = jnp.concatenate(
        [kpoint_grid, target_owner[None], target_slot[None], jnp.zeros((3, kpoints), jnp.int32)], 0
    )
    known = exchange(jnp.broadcast_to(own[None], (devices, 8, kpoints)))
    asked = known[:, 3] == me
    position = jnp.cumsum(asked.astype(jnp.int32), 1) - 1
    chosen = asked[:, None, :] & (position[:, None, :] == jnp.arange(capacity)[None, :, None])
    wanted = jnp.sum(jnp.where(chosen, known[:, 4][:, None, :], 0), 2)
    picked = eigen_vectors[wanted.reshape(-1)].reshape(devices, capacity * orbitals, lanes)
    fetched = exchange(picked).reshape(devices * capacity, orbitals, lanes)
    high, low = prepare_table(wannier_table)

    owners = (target_owner[:, None] == jnp.arange(devices, dtype=jnp.int32)[None, :]).astype(jnp.int32)
    before = jnp.cumsum(owners, 0) - owners
    far = fetched[target_owner * capacity + jnp.sum(before * owners, 1)]

    grid_rows = known.transpose(0, 2, 1).astype(jnp.float32)
    turned_rows = lax.dynamic_slice_in_dim(jnp.concatenate([grid_rows, grid_rows], 0), me, devices, 0)
    lattice_rows = jnp.concatenate([lattice, jnp.zeros((5, vectors), jnp.int32)], 0).astype(jnp.float32)
    cuts = [(0, kpoints // 4 * 3, by_shift), (kpoints // 4 * 3, kpoints, False)]
    sent = []
    for start, end, shifted in cuts:
        rows = (turned_rows if shifted else grid_rows)[:, start:end].reshape(devices * (end - start), 8)
        values = interpolate(rows, lattice_rows, high, low, mrows)
        values = values.reshape(devices, (end - start) * mrows, lanes)
        if shifted:
            sent.append(spread(lambda s: values[s], devices))
        elif tiled:
            sent.append([exchange(values)])
        else:
            got = exchange(values)
            got = got.reshape(devices, end - start, mrows, lanes)
            sent.append([got.transpose(1, 0, 2, 3).reshape(end - start, devices * mrows, lanes)])
    out = None
    place = me.astype(jnp.int32).reshape(1)
    for (start, end, shifted), pieces in zip(cuts, sent):
        out = rotate(pieces, eigen_vectors, far, mrows if tiled else 0, modes, start, place, out)
    return out


def solution(mesh):
    placed = (
        P(None, "grp", "ka"),
        P(None, "grp"),
        P(None, ("grp", "ka")),
        P(("grp", "ka"), None, None),
        P(("grp", "ka")),
        P(("grp", "ka")),
    )
    return jax.shard_map(
        placed_local,
        mesh=mesh,
        in_specs=placed,
        out_specs=P(("grp", "ka"), None, None, None),
        check_vma=False,
    )
```

```python
import math

import jax
import jax.numpy as jnp
from jax import lax
from jax.experimental import pallas as pl
from jax.experimental.pallas import tpu as pltpu
from jax.sharding import PartitionSpec as P


KMESH = 64
SHIFTED = 16

SIN_TERMS = [(-1.0) ** i * math.pi ** (2 * i + 1) / math.factorial(2 * i + 1) for i in range(7)]
COS_TERMS = [(-1.0) ** i * math.pi ** (2 * i) / math.factorial(2 * i) for i in range(8)]


def horner(terms, x):
    total = jnp.full_like(x, terms[-1])
    for term in terms[-2::-1]:
        total = total * x + term
    return total


def split(x):
    high = x.astype(jnp.bfloat16)
    return high, (x - high.astype(jnp.float32)).astype(jnp.bfloat16)


def dot(a, b):
    return jnp.dot(a, b, preferred_element_type=jnp.float32)


def dot3(a, b):
    return dot(a[0], b[0]) + dot(a[0], b[1]) + dot(a[1], b[0])


def table_kernel(table, high, low):
    half = pl.program_id(0)
    pairs = table.shape[2]
    lane = lax.broadcasted_iota(jnp.int32, (table.shape[1], 128), 1)
    first = lane < 64
    for block in range(pairs // 128):
        cut = slice(block * 128, (block + 1) * 128)

        def put(at, value):
            a, b = split(value)
            high[:, at * 128 : (at + 1) * 128] = a
            low[:, at * 128 : (at + 1) * 128] = b

        @pl.when(half == 0)
        def _():
            real, imag = table[0, :, cut], table[1, :, cut]
            put(2 * block, jnp.where(first, real, pltpu.roll(imag, 64, 1)))
            put(2 * block + 1, jnp.where(first, pltpu.roll(real, 64, 1), imag))

        @pl.when(half == 1)
        def _():
            real, imag = table[0, :, cut], table[1, :, cut]
            put(2 * block, jnp.where(first, -imag, pltpu.roll(real, 64, 1)))
            put(2 * block + 1, jnp.where(first, -pltpu.roll(imag, 64, 1), real))


def prepare_table(table):
    vectors, pairs = table.shape[1:]
    rows = min(vectors, 256)
    steps = vectors // rows
    return pl.pallas_call(
        table_kernel,
        out_shape=[jax.ShapeDtypeStruct((2 * vectors, 2 * pairs), jnp.bfloat16)] * 2,
        grid=(2, steps),
        in_specs=[pl.BlockSpec((2, rows, pairs), lambda h, i: (0, i, 0))],
        out_specs=[pl.BlockSpec((rows, 2 * pairs), lambda h, i: (h * steps + i, 0))] * 2,
        name="table",
    )(table)


def interpolate_kernel(grid_rows, lattice, high, low, out, *, mrows):
    turns = dot(grid_rows[...].astype(jnp.bfloat16), lattice[...].astype(jnp.bfloat16)) * (1.0 / KMESH)
    part = turns - jnp.round(turns)
    square = part * part
    sine = horner(SIN_TERMS, square) * part
    cosine = horner(COS_TERMS, square)
    phase = jnp.concatenate([1.0 - 2.0 * sine * sine, 2.0 * sine * cosine], 1)
    result = dot3(split(phase), (high[...], low[...]))
    rows = result.shape[0]
    for m in range(mrows):
        out[pl.ds(m, rows, stride=mrows), :] = result[:, m * 128 : (m + 1) * 128]


def interpolate(grid_rows, lattice, high, low, mrows):
    rows = grid_rows.shape[0]
    step = min(rows, 256)
    whole = lambda a: pl.BlockSpec(a.shape, lambda i: (0, 0))
    return pl.pallas_call(
        lambda *refs: interpolate_kernel(*refs, mrows=mrows),
        out_shape=jax.ShapeDtypeStruct((rows * mrows, 128), jnp.float32),
        grid=(rows // step,),
        in_specs=[
            pl.BlockSpec((step, grid_rows.shape[1]), lambda i: (i, 0)),
            whole(lattice),
            whole(high),
            whole(low),
        ],
        out_specs=pl.BlockSpec((step * mrows, 128), lambda i: (i, 0)),
        name="interpolate",
    )(grid_rows, lattice, high, low)


def rotate_one(values, u, far, orbitals):
    lanes = 2 * orbitals
    first = lax.broadcasted_iota(jnp.int32, (orbitals, lanes), 1) < orbitals
    first_all = lax.broadcasted_iota(jnp.int32, (values.shape[0], lanes), 1) < orbitals
    u_turned = pltpu.roll(u, orbitals, 1)
    u_full = jnp.concatenate([u, jnp.where(first, -u_turned, u_turned)], 0)
    right = dot3(split(values), split(u_full))
    turned = pltpu.roll(right, orbitals, 1)
    turned = jnp.where(first_all, turned, -turned)
    v = far.T
    left = jnp.concatenate([v[:orbitals], v[orbitals:]], 1)
    modes = values.shape[0] // orbitals
    by_mode = lambda x: jnp.concatenate([x[a * orbitals : (a + 1) * orbitals] for a in range(modes)], 1)
    done = dot3(split(left), split(jnp.concatenate([by_mode(right), by_mode(turned)], 0)))
    return [done[:, a * lanes : (a + 1) * lanes] for a in range(modes)]


def rotate_kernel(place, *refs, block, mrows, parts, orbitals):
    pieces = refs[:parts]
    near, far = refs[parts : parts + 2]
    out, gathered = refs[-2:]
    for k in range(block):
        if parts == 1 and mrows:
            values = pieces[0][:, k * mrows : (k + 1) * mrows, :].reshape(gathered.shape[1:])
        elif mrows:
            for s in range(parts):
                at = pl.multiple_of(lax.rem(place[0] + (parts - s), parts) * mrows, mrows)
                gathered[k, pl.ds(at, mrows), :] = pieces[s][k * mrows : (k + 1) * mrows, :]
            values = gathered[k]
        else:
            values = pieces[0][k]
        for a, done in enumerate(rotate_one(values, near[k], far[k], orbitals)):
            out[k, a] = done


def rotate(pieces, near, far, mrows, modes, start, place, before):
    total, orbitals = near.shape[:2]
    block = 8
    first = start // block
    lanes = 2 * orbitals
    if mrows and len(pieces) == 1:
        kpoints = pieces[0].shape[1] // mrows
        piece_spec = pl.BlockSpec((pieces[0].shape[0], block * mrows, lanes), lambda i, _: (0, i, 0))
    elif mrows:
        kpoints = pieces[0].shape[0] // mrows
        piece_spec = pl.BlockSpec((block * mrows, lanes), lambda i, _: (i, 0))
    else:
        kpoints = pieces[0].shape[0]
        piece_spec = pl.BlockSpec((block, modes * orbitals, lanes), lambda i, _: (i, 0, 0))
    prior = [] if before is None else [before]
    return pl.pallas_call(
        lambda *refs: rotate_kernel(
            *refs, block=block, mrows=mrows, parts=len(pieces), orbitals=orbitals
        ),
        out_shape=jax.ShapeDtypeStruct((total, modes, orbitals, lanes), jnp.float32),
        grid_spec=pltpu.PrefetchScalarGridSpec(
            num_scalar_prefetch=1,
            grid=(kpoints // block,),
            in_specs=[piece_spec] * len(pieces)
            + [
                pl.BlockSpec((block, orbitals, lanes), lambda i, _: (first + i, 0, 0)),
                pl.BlockSpec((block, orbitals, lanes), lambda i, _: (first + i, 0, 0)),
            ]
            + [pl.BlockSpec(memory_space=pl.ANY)] * len(prior),
            out_specs=pl.BlockSpec((block, modes, orbitals, lanes), lambda i, _: (first + i, 0, 0, 0)),
            scratch_shapes=[pltpu.VMEM((block, modes * orbitals, lanes), jnp.float32)],
        ),
        input_output_aliases={len(pieces) + 3: 0} if prior else {},
        name="rotate",
    )(place, *pieces, near, far, *prior)


def exchange(x):
    return lax.all_to_all(x, "ka", split_axis=0, concat_axis=0, tiled=True)


def shift_order(devices):
    far_first = sorted(range(1, devices), key=lambda s: -min(s, devices - s))
    order = []
    while far_first:
        order.append(far_first.pop(0))
        if far_first:
            order.append(far_first.pop())
    return order


def spread(blocks, devices):
    got = {0: blocks(0)}
    for s in shift_order(devices):
        got[s] = lax.ppermute(blocks(s), "ka", [(d, (d + s) % devices) for d in range(devices)])
    return [got[s] for s in range(devices)]


def placed_local(wannier_table, lattice, kpoint_grid, eigen_vectors, target_owner, target_slot):
    kpoints, orbitals = eigen_vectors.shape[:2]
    vectors, pairs = wannier_table.shape[1:]
    devices = lax.axis_size("ka")
    me = lax.axis_index("ka")
    mrows = pairs // orbitals
    modes = devices * mrows // orbitals
    lanes = 2 * orbitals
    capacity = 2 * kpoints // devices
    tiled = mrows % 8 == 0
    by_shift = devices <= SHIFTED and tiled

    half = devices // 2
    base = me // half * half
    away = lax.rem(me + half, devices)
    groups = [list(range(half)), list(range(half, devices))]

    mirrored = lax.ppermute(eigen_vectors, "ka", [(d, (d + half) % devices) for d in range(devices)])
    own = jnp.concatenate(
        [kpoint_grid, target_owner[None], target_slot[None], jnp.zeros((3, kpoints), jnp.int32)], 0
    )
    known = exchange(jnp.broadcast_to(own[None], (devices, 8, kpoints)))
    near_known = lax.dynamic_slice_in_dim(known, base, half, 0)

    def serve(held, owner):
        asked = near_known[:, 3] == owner
        position = jnp.cumsum(asked.astype(jnp.int32), 1) - 1
        chosen = asked[:, None, :] & (position[:, None, :] == jnp.arange(capacity)[None, :, None])
        wanted = jnp.sum(jnp.where(chosen, near_known[:, 4][:, None, :], 0), 2)
        picked = held[wanted.reshape(-1)].reshape(half, capacity * orbitals, lanes)
        got = lax.all_to_all(
            picked, "ka", split_axis=0, concat_axis=0, tiled=True, axis_index_groups=groups
        )
        return got.reshape(half * capacity, orbitals, lanes)

    from_near = serve(eigen_vectors, me)
    from_far = serve(mirrored, away)
    high, low = prepare_table(wannier_table)

    owners = (target_owner[:, None] == jnp.arange(devices, dtype=jnp.int32)[None, :]).astype(jnp.int32)
    before = jnp.cumsum(owners, 0) - owners
    at = lax.rem(target_owner, half) * capacity + jnp.sum(before * owners, 1)
    is_near = target_owner // half == me // half
    far = jnp.concatenate([from_near, from_far], 0)[jnp.where(is_near, at, at + half * capacity)]

    grid_rows = known.transpose(0, 2, 1).astype(jnp.float32)
    turned_rows = lax.dynamic_slice_in_dim(jnp.concatenate([grid_rows, grid_rows], 0), me, devices, 0)
    lattice_rows = jnp.concatenate([lattice, jnp.zeros((5, vectors), jnp.int32)], 0).astype(jnp.float32)
    cuts = [(0, kpoints // 4 * 3, by_shift), (kpoints // 4 * 3, kpoints, False)]
    sent = []
    for start, end, shifted in cuts:
        rows = (turned_rows if shifted else grid_rows)[:, start:end].reshape(devices * (end - start), 8)
        values = interpolate(rows, lattice_rows, high, low, mrows)
        values = values.reshape(devices, (end - start) * mrows, lanes)
        if shifted:
            sent.append(spread(lambda s: values[s], devices))
        elif tiled:
            sent.append([exchange(values)])
        else:
            got = exchange(values)
            got = got.reshape(devices, end - start, mrows, lanes)
            sent.append([got.transpose(1, 0, 2, 3).reshape(end - start, devices * mrows, lanes)])
    out = None
    place = me.astype(jnp.int32).reshape(1)
    for (start, end, shifted), pieces in zip(cuts, sent):
        out = rotate(pieces, eigen_vectors, far, mrows if tiled else 0, modes, start, place, out)
    return out


def solution(mesh):
    placed = (
        P(None, "grp", "ka"),
        P(None, "grp"),
        P(None, ("grp", "ka")),
        P(("grp", "ka"), None, None),
        P(("grp", "ka")),
        P(("grp", "ka")),
    )
    return jax.shard_map(
        placed_local,
        mesh=mesh,
        in_specs=placed,
        out_specs=P(("grp", "ka"), None, None, None),
        check_vma=False,
    )
```

```python
import math

import jax
import jax.numpy as jnp
from jax import lax
from jax.experimental import pallas as pl
from jax.experimental.pallas import tpu as pltpu
from jax.sharding import PartitionSpec as P


KMESH = 64
SHIFTED = 16

SIN_TERMS = [(-1.0) ** i * math.pi ** (2 * i + 1) / math.factorial(2 * i + 1) for i in range(7)]
COS_TERMS = [(-1.0) ** i * math.pi ** (2 * i) / math.factorial(2 * i) for i in range(8)]


def horner(terms, x):
    total = jnp.full_like(x, terms[-1])
    for term in terms[-2::-1]:
        total = total * x + term
    return total


def split(x):
    high = x.astype(jnp.bfloat16)
    return high, (x - high.astype(jnp.float32)).astype(jnp.bfloat16)


def dot(a, b):
    return jnp.dot(a, b, preferred_element_type=jnp.float32)


def dot3(a, b):
    return dot(a[0], b[0]) + dot(a[0], b[1]) + dot(a[1], b[0])


def table_kernel(table, high, low):
    half = pl.program_id(0)
    pairs = table.shape[2]
    lane = lax.broadcasted_iota(jnp.int32, (table.shape[1], 128), 1)
    first = lane < 64
    for block in range(pairs // 128):
        cut = slice(block * 128, (block + 1) * 128)

        def put(at, value):
            a, b = split(value)
            high[:, at * 128 : (at + 1) * 128] = a
            low[:, at * 128 : (at + 1) * 128] = b

        @pl.when(half == 0)
        def _():
            real, imag = table[0, :, cut], table[1, :, cut]
            put(2 * block, jnp.where(first, real, pltpu.roll(imag, 64, 1)))
            put(2 * block + 1, jnp.where(first, pltpu.roll(real, 64, 1), imag))

        @pl.when(half == 1)
        def _():
            real, imag = table[0, :, cut], table[1, :, cut]
            put(2 * block, jnp.where(first, -imag, pltpu.roll(real, 64, 1)))
            put(2 * block + 1, jnp.where(first, -pltpu.roll(imag, 64, 1), real))


def prepare_table(table):
    vectors, pairs = table.shape[1:]
    rows = min(vectors, 256)
    steps = vectors // rows
    return pl.pallas_call(
        table_kernel,
        out_shape=[jax.ShapeDtypeStruct((2 * vectors, 2 * pairs), jnp.bfloat16)] * 2,
        grid=(2, steps),
        in_specs=[pl.BlockSpec((2, rows, pairs), lambda h, i: (0, i, 0))],
        out_specs=[pl.BlockSpec((rows, 2 * pairs), lambda h, i: (h * steps + i, 0))] * 2,
        name="table",
    )(table)


def interpolate_kernel(grid_rows, lattice, high, low, out, *, mrows):
    turns = dot(grid_rows[...].astype(jnp.bfloat16), lattice[...].astype(jnp.bfloat16)) * (1.0 / KMESH)
    part = turns - jnp.round(turns)
    square = part * part
    sine = horner(SIN_TERMS, square) * part
    cosine = horner(COS_TERMS, square)
    phase = jnp.concatenate([1.0 - 2.0 * sine * sine, 2.0 * sine * cosine], 1)
    result = dot3(split(phase), (high[...], low[...]))
    rows = result.shape[0]
    for m in range(mrows):
        out[pl.ds(m, rows, stride=mrows), :] = result[:, m * 128 : (m + 1) * 128]


def interpolate(grid_rows, lattice, high, low, mrows):
    rows = grid_rows.shape[0]
    step = max(n for n in range(8, 257, 8) if rows % n == 0)
    whole = lambda a: pl.BlockSpec(a.shape, lambda i: (0, 0))
    return pl.pallas_call(
        lambda *refs: interpolate_kernel(*refs, mrows=mrows),
        out_shape=jax.ShapeDtypeStruct((rows * mrows, 128), jnp.float32),
        grid=(rows // step,),
        in_specs=[
            pl.BlockSpec((step, grid_rows.shape[1]), lambda i: (i, 0)),
            whole(lattice),
            whole(high),
            whole(low),
        ],
        out_specs=pl.BlockSpec((step * mrows, 128), lambda i: (i, 0)),
        name="interpolate",
    )(grid_rows, lattice, high, low)


def rotate_one(values, u, far, orbitals):
    lanes = 2 * orbitals
    first = lax.broadcasted_iota(jnp.int32, (orbitals, lanes), 1) < orbitals
    first_all = lax.broadcasted_iota(jnp.int32, (values.shape[0], lanes), 1) < orbitals
    u_turned = pltpu.roll(u, orbitals, 1)
    u_full = jnp.concatenate([u, jnp.where(first, -u_turned, u_turned)], 0)
    right = dot3(split(values), split(u_full))
    turned = pltpu.roll(right, orbitals, 1)
    turned = jnp.where(first_all, turned, -turned)
    v = far.T
    left = jnp.concatenate([v[:orbitals], v[orbitals:]], 1)
    modes = values.shape[0] // orbitals
    by_mode = lambda x: jnp.concatenate([x[a * orbitals : (a + 1) * orbitals] for a in range(modes)], 1)
    done = dot3(split(left), split(jnp.concatenate([by_mode(right), by_mode(turned)], 0)))
    return [done[:, a * lanes : (a + 1) * lanes] for a in range(modes)]


def rotate_kernel(place, *refs, block, mrows, parts, orbitals):
    pieces = refs[:parts]
    near, far = refs[parts : parts + 2]
    out, gathered = refs[-2:]
    for k in range(block):
        if parts == 1 and mrows:
            values = pieces[0][:, k * mrows : (k + 1) * mrows, :].reshape(gathered.shape[1:])
        elif mrows:
            for s in range(parts):
                at = pl.multiple_of(lax.rem(place[0] + (parts - s), parts) * mrows, mrows)
                gathered[k, pl.ds(at, mrows), :] = pieces[s][k * mrows : (k + 1) * mrows, :]
            values = gathered[k]
        else:
            values = pieces[0][k]
        for a, done in enumerate(rotate_one(values, near[k], far[k], orbitals)):
            out[k, a] = done


def rotate(pieces, near, far, mrows, modes, start, place, before):
    total, orbitals = near.shape[:2]
    block = 8
    first = start // block
    lanes = 2 * orbitals
    if mrows and len(pieces) == 1:
        kpoints = pieces[0].shape[1] // mrows
        piece_spec = pl.BlockSpec((pieces[0].shape[0], block * mrows, lanes), lambda i, _: (0, i, 0))
    elif mrows:
        kpoints = pieces[0].shape[0] // mrows
        piece_spec = pl.BlockSpec((block * mrows, lanes), lambda i, _: (i, 0))
    else:
        kpoints = pieces[0].shape[0]
        piece_spec = pl.BlockSpec((block, modes * orbitals, lanes), lambda i, _: (i, 0, 0))
    prior = [] if before is None else [before]
    return pl.pallas_call(
        lambda *refs: rotate_kernel(
            *refs, block=block, mrows=mrows, parts=len(pieces), orbitals=orbitals
        ),
        out_shape=jax.ShapeDtypeStruct((total, modes, orbitals, lanes), jnp.float32),
        grid_spec=pltpu.PrefetchScalarGridSpec(
            num_scalar_prefetch=1,
            grid=(kpoints // block,),
            in_specs=[piece_spec] * len(pieces)
            + [
                pl.BlockSpec((block, orbitals, lanes), lambda i, _: (first + i, 0, 0)),
                pl.BlockSpec((block, orbitals, lanes), lambda i, _: (first + i, 0, 0)),
            ]
            + [pl.BlockSpec(memory_space=pl.ANY)] * len(prior),
            out_specs=pl.BlockSpec((block, modes, orbitals, lanes), lambda i, _: (first + i, 0, 0, 0)),
            scratch_shapes=[pltpu.VMEM((block, modes * orbitals, lanes), jnp.float32)],
        ),
        input_output_aliases={len(pieces) + 3: 0} if prior else {},
        name="rotate",
    )(place, *pieces, near, far, *prior)


def exchange(x):
    return lax.all_to_all(x, "ka", split_axis=0, concat_axis=0, tiled=True)


def shift_order(devices):
    far_first = sorted(range(1, devices), key=lambda s: -min(s, devices - s))
    order = []
    while far_first:
        order.append(far_first.pop(0))
        if far_first:
            order.append(far_first.pop())
    return order


def spread(blocks, devices):
    got = {0: blocks(0)}
    for s in shift_order(devices):
        got[s] = lax.ppermute(blocks(s), "ka", [(d, (d + s) % devices) for d in range(devices)])
    return [got[s] for s in range(devices)]


def placed_local(wannier_table, lattice, kpoint_grid, eigen_vectors, target_owner, target_slot):
    kpoints, orbitals = eigen_vectors.shape[:2]
    vectors, pairs = wannier_table.shape[1:]
    devices = lax.axis_size("ka")
    me = lax.axis_index("ka")
    mrows = pairs // orbitals
    modes = devices * mrows // orbitals
    lanes = 2 * orbitals
    capacity = 2 * kpoints // devices
    tiled = mrows % 8 == 0
    by_shift = devices <= SHIFTED and tiled

    own = jnp.concatenate(
        [kpoint_grid, target_owner[None], target_slot[None], jnp.zeros((3, kpoints), jnp.int32)], 0
    )
    known = exchange(jnp.broadcast_to(own[None], (devices, 8, kpoints)))
    asked = known[:, 3] == me
    position = jnp.cumsum(asked.astype(jnp.int32), 1) - 1
    chosen = asked[:, None, :] & (position[:, None, :] == jnp.arange(capacity)[None, :, None])
    wanted = jnp.sum(jnp.where(chosen, known[:, 4][:, None, :], 0), 2)
    picked = eigen_vectors[wanted.reshape(-1)].reshape(devices, capacity * orbitals, lanes)
    fetched = exchange(picked).reshape(devices * capacity, orbitals, lanes)
    high, low = prepare_table(wannier_table)

    owners = (target_owner[:, None] == jnp.arange(devices, dtype=jnp.int32)[None, :]).astype(jnp.int32)
    before = jnp.cumsum(owners, 0) - owners
    far = fetched[target_owner * capacity + jnp.sum(before * owners, 1)]

    grid_rows = known.transpose(0, 2, 1).astype(jnp.float32)
    turned_rows = lax.dynamic_slice_in_dim(jnp.concatenate([grid_rows, grid_rows], 0), me, devices, 0)
    lattice_rows = jnp.concatenate([lattice, jnp.zeros((5, vectors), jnp.int32)], 0).astype(jnp.float32)
    edges = [0, kpoints // 2, kpoints // 8 * 7, kpoints]
    cuts = [(start, end, by_shift and c != 2) for c, (start, end) in enumerate(zip(edges, edges[1:]))]
    sent = []
    for start, end, shifted in cuts:
        rows = (turned_rows if shifted else grid_rows)[:, start:end].reshape(devices * (end - start), 8)
        values = interpolate(rows, lattice_rows, high, low, mrows)
        values = values.reshape(devices, (end - start) * mrows, lanes)
        if shifted:
            sent.append(spread(lambda s: values[s], devices))
        elif tiled:
            sent.append([exchange(values)])
        else:
            got = exchange(values)
            got = got.reshape(devices, end - start, mrows, lanes)
            sent.append([got.transpose(1, 0, 2, 3).reshape(end - start, devices * mrows, lanes)])
    out = None
    place = me.astype(jnp.int32).reshape(1)
    for c, pieces in enumerate(sent):
        out = rotate(pieces, eigen_vectors, far, mrows if tiled else 0, modes, edges[c], place, out)
    return out


def solution(mesh):
    placed = (
        P(None, "grp", "ka"),
        P(None, "grp"),
        P(None, ("grp", "ka")),
        P(("grp", "ka"), None, None),
        P(("grp", "ka")),
        P(("grp", "ka")),
    )
    return jax.shard_map(
        placed_local,
        mesh=mesh,
        in_specs=placed,
        out_specs=P(("grp", "ka"), None, None, None),
        check_vma=False,
    )
```

```python
import math

import jax
import jax.numpy as jnp
from jax import lax
from jax.experimental import pallas as pl
from jax.experimental.pallas import tpu as pltpu
from jax.sharding import PartitionSpec as P


KMESH = 64
RELAYED = 16
CROSSING = 48
FORCE = 0
LEADING = 2

SIN_TERMS = [(-1.0) ** i * math.pi ** (2 * i + 1) / math.factorial(2 * i + 1) for i in range(7)]
COS_TERMS = [(-1.0) ** i * math.pi ** (2 * i) / math.factorial(2 * i) for i in range(8)]


def horner(terms, x):
    total = jnp.full_like(x, terms[-1])
    for term in terms[-2::-1]:
        total = total * x + term
    return total


def split(x):
    high = x.astype(jnp.bfloat16)
    return high, (x - high.astype(jnp.float32)).astype(jnp.bfloat16)


def dot(a, b):
    return jnp.dot(a, b, preferred_element_type=jnp.float32)


def dot3(a, b):
    return dot(a[0], b[0]) + dot(a[0], b[1]) + dot(a[1], b[0])


def table_kernel(table, high, low):
    lane = lax.broadcasted_iota(jnp.int32, (table.shape[1], 128), 1)
    first = lane < 64

    def put(half, at, value):
        a, b = split(value)
        high[half, :, at * 128 : (at + 1) * 128] = a
        low[half, :, at * 128 : (at + 1) * 128] = b

    for block in range(table.shape[2] // 128):
        cut = slice(block * 128, (block + 1) * 128)
        real, imag = table[0, :, cut], table[1, :, cut]
        real_turned, imag_turned = pltpu.roll(real, 64, 1), pltpu.roll(imag, 64, 1)
        put(0, 2 * block, jnp.where(first, real, imag_turned))
        put(0, 2 * block + 1, jnp.where(first, real_turned, imag))
        put(1, 2 * block, jnp.where(first, -imag, real_turned))
        put(1, 2 * block + 1, jnp.where(first, -imag_turned, real))


def prepare_table(table):
    vectors, pairs = table.shape[1:]
    rows = math.gcd(vectors, 128)
    high, low = pl.pallas_call(
        table_kernel,
        out_shape=[jax.ShapeDtypeStruct((2, vectors, 2 * pairs), jnp.bfloat16)] * 2,
        grid=(vectors // rows,),
        in_specs=[pl.BlockSpec((2, rows, pairs), lambda i: (0, i, 0))],
        out_specs=[pl.BlockSpec((2, rows, 2 * pairs), lambda i: (0, i, 0))] * 2,
        name="table",
    )(table)
    return high.reshape(2 * vectors, 2 * pairs), low.reshape(2 * vectors, 2 * pairs)


def interpolate_kernel(grid_rows, lattice, high, low, *refs, mrows, parts):
    outs = refs[-parts:]
    turns = dot(grid_rows[...].astype(jnp.bfloat16), lattice[...].astype(jnp.bfloat16)) * (1.0 / KMESH)
    part = turns - jnp.round(turns)
    square = part * part
    sine = horner(SIN_TERMS, square) * part
    cosine = horner(COS_TERMS, square)
    phase = jnp.concatenate([1.0 - 2.0 * sine * sine, 2.0 * sine * cosine], 1)
    result = dot3(split(phase), (high[...], low[...]))
    rows = result.shape[0]

    def store(out, first, count):
        for m in range(mrows):
            out[pl.ds(m, count, stride=mrows), :] = result[first : first + count, m * 128 : (m + 1) * 128]

    if parts == 1:
        store(outs[0], 0, rows)
        return
    each = outs[0].shape[0] // mrows
    per_step = rows // each
    for i in range(parts // per_step):

        @pl.when(pl.program_id(0) == i)
        def _():
            for j in range(per_step):
                store(outs[i * per_step + j], j * each, each)


def interpolate(grid_rows, lattice, high, low, mrows, parts, ready):
    rows = grid_rows.shape[0]
    unit = rows // parts if parts > 1 else 8
    step = max(n for n in range(unit, 257, unit) if rows % n == 0)
    whole = lambda a: pl.BlockSpec(a.shape, lambda i: (0, 0))
    if parts == 1:
        out_specs = [pl.BlockSpec((step * mrows, 128), lambda i: (i, 0))]
    else:
        out_specs = [pl.BlockSpec((unit * mrows, 128), lambda i: (0, 0))] * parts
    return pl.pallas_call(
        lambda *refs: interpolate_kernel(*refs, mrows=mrows, parts=parts),
        out_shape=[jax.ShapeDtypeStruct((rows // parts * mrows, 128), jnp.float32)] * parts,
        grid=(rows // step,),
        in_specs=[
            pl.BlockSpec((step, grid_rows.shape[1]), lambda i: (i, 0)),
            whole(lattice),
            whole(high),
            whole(low),
        ]
        + [pl.BlockSpec(memory_space=pl.ANY)] * len(ready),
        out_specs=out_specs,
        name="interpolate",
    )(grid_rows, lattice, high, low, *ready)


def rotate_one(values, u, far, orbitals):
    lanes = 2 * orbitals
    first = lax.broadcasted_iota(jnp.int32, (orbitals, lanes), 1) < orbitals
    first_all = lax.broadcasted_iota(jnp.int32, (values.shape[0], lanes), 1) < orbitals
    u_turned = pltpu.roll(u, orbitals, 1)
    u_full = jnp.concatenate([u, jnp.where(first, -u_turned, u_turned)], 0)
    right = dot3(split(values), split(u_full))
    turned = pltpu.roll(right, orbitals, 1)
    turned = jnp.where(first_all, turned, -turned)
    v = far.T
    left = jnp.concatenate([v[:orbitals], v[orbitals:]], 1)
    modes = values.shape[0] // orbitals
    by_mode = lambda x: jnp.concatenate([x[a * orbitals : (a + 1) * orbitals] for a in range(modes)], 1)
    done = dot3(split(left), split(jnp.concatenate([by_mode(right), by_mode(turned)], 0)))
    return [done[:, a * lanes : (a + 1) * lanes] for a in range(modes)]


def rotate_kernel(place, far_at, *refs, block, mrows, parts, stores, held, start):
    pieces = refs[:parts]
    near = refs[parts]
    far_stores = refs[parts + 1 : parts + 1 + stores * block]
    out, gathered = refs[-2:]
    orbitals = near.shape[1]
    for k in range(block):
        if parts == 1 and mrows:
            values = pieces[0][:, k * mrows : (k + 1) * mrows, :].reshape(gathered.shape[1:])
        elif mrows:
            for s in range(parts):
                at = pl.multiple_of((place[0] ^ s) * mrows, mrows)
                gathered[k, pl.ds(at, mrows), :] = pieces[s][k * mrows : (k + 1) * mrows, :]
            values = gathered[k]
        else:
            values = pieces[0][k]
        at = far_at[start + pl.program_id(0) * block + k]
        far = far_stores[k][0]
        for n in range(1, stores):
            far = jnp.where(at >= n * held, far_stores[n * block + k][0], far)
        for a, done in enumerate(rotate_one(values, near[k], far, orbitals)):
            out[k, a] = done


def rotate(pieces, near, far_stores, far_at, mrows, modes, start, place, before):
    total, orbitals = near.shape[:2]
    block = 8
    first = start // block
    lanes = 2 * orbitals
    if mrows and len(pieces) == 1:
        kpoints = pieces[0].shape[1] // mrows
        piece_spec = pl.BlockSpec((pieces[0].shape[0], block * mrows, lanes), lambda i, *_: (0, i, 0))
    elif mrows:
        kpoints = pieces[0].shape[0] // mrows
        piece_spec = pl.BlockSpec((block * mrows, lanes), lambda i, *_: (i, 0))
    else:
        kpoints = pieces[0].shape[0]
        piece_spec = pl.BlockSpec((block, modes * orbitals, lanes), lambda i, *_: (i, 0, 0))
    prior = [] if before is None else [before]
    stores = len(far_stores)
    held = far_stores[0].shape[0]

    def far_spec(k):
        return pl.BlockSpec(
            (1, orbitals, lanes), lambda i, _, at: (lax.rem(at[start + i * block + k], held), 0, 0)
        )

    return pl.pallas_call(
        lambda *refs: rotate_kernel(
            *refs, block=block, mrows=mrows, parts=len(pieces), stores=stores, held=held, start=start
        ),
        out_shape=jax.ShapeDtypeStruct((total, modes, orbitals, lanes), jnp.float32),
        grid_spec=pltpu.PrefetchScalarGridSpec(
            num_scalar_prefetch=2,
            grid=(kpoints // block,),
            in_specs=[piece_spec] * len(pieces)
            + [pl.BlockSpec((block, orbitals, lanes), lambda i, *_: (first + i, 0, 0))]
            + [far_spec(k) for k in range(block)] * stores
            + [pl.BlockSpec(memory_space=pl.ANY)] * len(prior),
            out_specs=pl.BlockSpec((block, modes, orbitals, lanes), lambda i, *_: (first + i, 0, 0, 0)),
            scratch_shapes=[pltpu.VMEM((block, modes * orbitals, lanes), jnp.float32)],
        ),
        input_output_aliases={len(pieces) + stores * block + 3: 0} if prior else {},
        name="rotate",
    )(place, far_at, *pieces, near, *[x for x in far_stores for _ in range(block)], *prior)


def exchange(x):
    return lax.all_to_all(x, "ka", split_axis=0, concat_axis=0, tiled=True)


def send(blocks, patterns, devices):
    return [lax.ppermute(blocks[s], "ka", [(d, d ^ s) for d in range(devices)]) for s in patterns]


def picks(asked, value, capacity):
    position = jnp.cumsum(asked.astype(jnp.int32), -1) - 1
    chosen = asked[..., None, :] & (position[..., None, :] == jnp.arange(capacity)[:, None])
    return jnp.sum(jnp.where(chosen, value[..., None, :], 0), -1)


def rank(owner, devices):
    same = (owner[:, None] == jnp.arange(devices, dtype=jnp.int32)[None, :]).astype(jnp.int32)
    return jnp.sum((jnp.cumsum(same, 0) - same) * same, 1)


def placed_local(wannier_table, lattice, kpoint_grid, eigen_vectors, target_owner, target_slot):
    kpoints, orbitals = eigen_vectors.shape[:2]
    vectors, pairs = wannier_table.shape[1:]
    devices = lax.axis_size("ka")
    groups = lax.axis_size("grp")
    me = lax.axis_index("ka")
    mrows = pairs // orbitals
    modes = devices * mrows // orbitals
    lanes = 2 * orbitals
    capacity = 2 * kpoints // devices
    tiled = mrows % 8 == 0
    relayed = devices <= RELAYED and devices & (devices - 1) == 0 and tiled
    place = me.astype(jnp.int32).reshape(1)
    lattice_rows = jnp.concatenate([lattice, jnp.zeros((5, vectors), jnp.int32)], 0).astype(jnp.float32)

    own = jnp.concatenate(
        [kpoint_grid, target_owner[None], target_slot[None], jnp.zeros((3, kpoints), jnp.int32)], 0
    )
    everyone = lax.all_to_all(
        jnp.broadcast_to(own[None], (groups * devices, 8, kpoints)),
        ("grp", "ka"),
        split_axis=0,
        concat_axis=0,
        tiled=True,
    ).reshape(groups, devices, 8, kpoints)
    known = lax.dynamic_index_in_dim(everyone, lax.axis_index("grp"), 0, keepdims=False)
    far_rank = rank(target_owner, devices)

    def fill(rows, high, low, parts, ready=()):
        count = rows.shape[0] * rows.shape[1]
        return interpolate(rows.reshape(count, 8), lattice_rows, high, low, mrows, parts, ready)

    def plain():
        wanted = picks(known[:, 3] == me, known[:, 4], capacity)
        picked = eigen_vectors[wanted.reshape(-1)].reshape(devices, capacity * orbitals, lanes)
        fetched = exchange(picked).reshape(devices * capacity, orbitals, lanes)
        far_at = target_owner * capacity + far_rank
        high, low = prepare_table(wannier_table)
        [values] = fill(known.transpose(0, 2, 1).astype(jnp.float32), high, low, 1)
        pieces = exchange(values.reshape(devices, kpoints * mrows, lanes))
        if not tiled:
            pieces = pieces.reshape(devices, kpoints, mrows, lanes).transpose(1, 0, 2, 3)
            pieces = pieces.reshape(kpoints, devices * mrows, lanes)
        mrows_or_none = mrows if tiled else 0
        return rotate([pieces], eigen_vectors, [fetched], far_at, mrows_or_none, modes, 0, place, None)

    if not relayed:
        return plain()

    half = devices // 2
    side = me // half
    mirror = me ^ half
    in_half = [list(range(half)), list(range(half, devices))]
    near_known = lax.dynamic_slice_in_dim(known, side * half, half, 0)
    away_known = lax.dynamic_slice_in_dim(known, (1 - side) * half, half, 0)
    side_of = jnp.arange(devices, dtype=jnp.int32)[None, :, None] // half
    crossing = everyone[:, :, 3] // half != side_of
    owners = jnp.arange(devices, dtype=jnp.int32)
    counts = jnp.sum(
        (crossing & (everyone[:, :, 3] == owners[:, None, None, None])).astype(jnp.int32), (2, 3)
    )
    fits = jnp.max(counts) <= CROSSING * kpoints // 64

    def serve(held, wanted):
        picked = held[wanted.reshape(-1)].reshape(half, capacity * orbitals, lanes)
        got = lax.all_to_all(
            picked, "ka", split_axis=0, concat_axis=0, tiled=True, axis_index_groups=in_half
        )
        return got.reshape(half * capacity, orbitals, lanes)

    def asked_slots(block, owner):
        hit = (block[:, 3] == owner)[..., None] & (block[:, 4][..., None] == jnp.arange(kpoints))
        return jnp.any(hit, (0, 1))

    def relay(room):
        slots = jnp.arange(kpoints, dtype=jnp.int32)
        leaving = picks(asked_slots(away_known, me), slots, room)
        mirrored = lax.ppermute(
            eigen_vectors[leaving], "ka", [(d, d ^ half) for d in range(devices)]
        )
        from_near = serve(eigen_vectors, picks(near_known[:, 3] == me, near_known[:, 4], capacity))
        arrived = jnp.cumsum(asked_slots(near_known, mirror).astype(jnp.int32)) - 1
        at_slot = near_known[:, 4][..., None] == slots
        row_of = jnp.sum(jnp.where(at_slot, arrived, 0), -1)
        from_far = serve(mirrored, picks(near_known[:, 3] == mirror, row_of, capacity))

        at = target_owner % half * capacity + far_rank
        far_at = jnp.where(target_owner // half == side, at, at + half * capacity)

        high, low = prepare_table(wannier_table)
        grid_rows = known.transpose(0, 2, 1).astype(jnp.float32)
        turned_rows = grid_rows[me ^ owners]
        edges = [0, kpoints // 2, kpoints // 4 * 3, kpoints]
        sent = []
        for start, end in zip(edges, edges[1:]):
            last = end == kpoints
            rows = (grid_rows if last else turned_rows)[:, start:end]
            values = fill(rows, high, low, 1 if last else devices, [far_at])
            if last:
                sent.append([exchange(values[0].reshape(devices, (end - start) * mrows, lanes))])
            else:
                crossed = send(values, range(half, half + LEADING), devices)
                crossed += send(values, range(half + LEADING, devices), devices)
                sent.append([values[0]] + send(values, range(1, half), devices) + crossed)

        out = None
        for c, pieces in enumerate(sent):
            out = rotate(
                pieces, eigen_vectors, [from_near, from_far], far_at, mrows, modes, edges[c], place, out
            )
        return out

    if FORCE:
        return relay(FORCE)
    return lax.cond(fits, lambda: relay(CROSSING * kpoints // 64), plain)


def solution(mesh):
    placed = (
        P(None, "grp", "ka"),
        P(None, "grp"),
        P(None, ("grp", "ka")),
        P(("grp", "ka"), None, None),
        P(("grp", "ka")),
        P(("grp", "ka")),
    )
    return jax.shard_map(
        placed_local,
        mesh=mesh,
        in_specs=placed,
        out_specs=P(("grp", "ka"), None, None, None),
        check_vma=False,
    )
```

```python
import math

import jax
import jax.numpy as jnp
from jax import lax
from jax.experimental import pallas as pl
from jax.experimental.pallas import tpu as pltpu
from jax.sharding import PartitionSpec as P


KMESH = 64
RELAYED = 16
CROSSING = 48
FORCE = 0
LEADING = 2

SIN_TERMS = [(-1.0) ** i * math.pi ** (2 * i + 1) / math.factorial(2 * i + 1) for i in range(7)]
COS_TERMS = [(-1.0) ** i * math.pi ** (2 * i) / math.factorial(2 * i) for i in range(8)]


def horner(terms, x):
    total = jnp.full_like(x, terms[-1])
    for term in terms[-2::-1]:
        total = total * x + term
    return total


def split(x):
    high = x.astype(jnp.bfloat16)
    return high, (x - high.astype(jnp.float32)).astype(jnp.bfloat16)


def dot(a, b):
    return jnp.dot(a, b, preferred_element_type=jnp.float32)


def dot3(a, b):
    return dot(a[0], b[0]) + dot(a[0], b[1]) + dot(a[1], b[0])


def table_kernel(table, high, low):
    lane = lax.broadcasted_iota(jnp.int32, (table.shape[1], 128), 1)
    first = lane < 64

    def put(half, at, value):
        a, b = split(value)
        high[half, :, at * 128 : (at + 1) * 128] = a
        low[half, :, at * 128 : (at + 1) * 128] = b

    for block in range(table.shape[2] // 128):
        cut = slice(block * 128, (block + 1) * 128)
        real, imag = table[0, :, cut], table[1, :, cut]
        real_turned, imag_turned = pltpu.roll(real, 64, 1), pltpu.roll(imag, 64, 1)
        put(0, 2 * block, jnp.where(first, real, imag_turned))
        put(0, 2 * block + 1, jnp.where(first, real_turned, imag))
        put(1, 2 * block, jnp.where(first, -imag, real_turned))
        put(1, 2 * block + 1, jnp.where(first, -imag_turned, real))


def prepare_table(table):
    vectors, pairs = table.shape[1:]
    rows = math.gcd(vectors, 128)
    high, low = pl.pallas_call(
        table_kernel,
        out_shape=[jax.ShapeDtypeStruct((2, vectors, 2 * pairs), jnp.bfloat16)] * 2,
        grid=(vectors // rows,),
        in_specs=[pl.BlockSpec((2, rows, pairs), lambda i: (0, i, 0))],
        out_specs=[pl.BlockSpec((2, rows, 2 * pairs), lambda i: (0, i, 0))] * 2,
        name="table",
    )(table)
    return high.reshape(2 * vectors, 2 * pairs), low.reshape(2 * vectors, 2 * pairs)


def interpolate_kernel(grid_rows, lattice, high, low, *refs, mrows, parts):
    outs = refs[-parts:]
    turns = dot(grid_rows[...].astype(jnp.bfloat16), lattice[...].astype(jnp.bfloat16)) * (1.0 / KMESH)
    part = turns - jnp.round(turns)
    square = part * part
    sine = horner(SIN_TERMS, square) * part
    cosine = horner(COS_TERMS, square)
    phase = jnp.concatenate([1.0 - 2.0 * sine * sine, 2.0 * sine * cosine], 1)
    result = dot3(split(phase), (high[...], low[...]))
    rows = result.shape[0]

    def store(out, first, count):
        for m in range(mrows):
            out[pl.ds(m, count, stride=mrows), :] = result[first : first + count, m * 128 : (m + 1) * 128]

    if parts == 1:
        store(outs[0], 0, rows)
        return
    each = outs[0].shape[0] // mrows
    per_step = rows // each
    for i in range(parts // per_step):

        @pl.when(pl.program_id(0) == i)
        def _():
            for j in range(per_step):
                store(outs[i * per_step + j], j * each, each)


def interpolate(grid_rows, lattice, high, low, mrows, parts, ready):
    rows = grid_rows.shape[0]
    unit = rows // parts if parts > 1 else 8
    step = max(n for n in range(unit, 257, unit) if rows % n == 0)
    whole = lambda a: pl.BlockSpec(a.shape, lambda i: (0, 0))
    if parts == 1:
        out_specs = [pl.BlockSpec((step * mrows, 128), lambda i: (i, 0))]
    else:
        out_specs = [pl.BlockSpec((unit * mrows, 128), lambda i: (0, 0))] * parts
    return pl.pallas_call(
        lambda *refs: interpolate_kernel(*refs, mrows=mrows, parts=parts),
        out_shape=[jax.ShapeDtypeStruct((rows // parts * mrows, 128), jnp.float32)] * parts,
        grid=(rows // step,),
        in_specs=[
            pl.BlockSpec((step, grid_rows.shape[1]), lambda i: (i, 0)),
            whole(lattice),
            whole(high),
            whole(low),
        ]
        + [pl.BlockSpec(memory_space=pl.ANY)] * len(ready),
        out_specs=out_specs,
        name="interpolate",
    )(grid_rows, lattice, high, low, *ready)


def right_turn(values, u):
    orbitals, lanes = u.shape
    first = lax.broadcasted_iota(jnp.int32, (orbitals, lanes), 1) < orbitals
    u_turned = pltpu.roll(u, orbitals, 1)
    u_full = jnp.concatenate([u, jnp.where(first, -u_turned, u_turned)], 0)
    return dot3(split(values), split(u_full))


def left_turn(right, far):
    orbitals, lanes = far.shape
    first = lax.broadcasted_iota(jnp.int32, right.shape, 1) < orbitals
    turned = pltpu.roll(right, orbitals, 1)
    turned = jnp.where(first, turned, -turned)
    v = far.T
    left = jnp.concatenate([v[:orbitals], v[orbitals:]], 1)
    modes = right.shape[0] // orbitals
    by_mode = lambda x: jnp.concatenate([x[a * orbitals : (a + 1) * orbitals] for a in range(modes)], 1)
    done = dot3(split(left), split(jnp.concatenate([by_mode(right), by_mode(turned)], 0)))
    return [done[:, a * lanes : (a + 1) * lanes] for a in range(modes)]


def collect(place, pieces, gathered, k, mrows):
    parts = len(pieces)
    if not mrows:
        return pieces[0][k]
    if parts == 1:
        return pieces[0][:, k * mrows : (k + 1) * mrows, :].reshape(gathered.shape[1:])
    for s in range(parts):
        at = pl.multiple_of((place[0] ^ s) * mrows, mrows)
        gathered[k, pl.ds(at, mrows), :] = pieces[s][k * mrows : (k + 1) * mrows, :]
    return gathered[k]


def right_kernel(place, *refs, block, mrows, parts):
    near, out, gathered = refs[parts:]
    for k in range(block):
        out[k] = right_turn(collect(place, refs[:parts], gathered, k, mrows), near[k])


def turn_right(pieces, near, mrows, rows, start, place):
    lanes = near.shape[2]
    block = 8
    first = start // block
    kpoints = pieces[0].shape[0] // mrows
    return pl.pallas_call(
        lambda *refs: right_kernel(*refs, block=block, mrows=mrows, parts=len(pieces)),
        out_shape=jax.ShapeDtypeStruct((kpoints, rows, lanes), jnp.float32),
        grid_spec=pltpu.PrefetchScalarGridSpec(
            num_scalar_prefetch=1,
            grid=(kpoints // block,),
            in_specs=[pl.BlockSpec((block * mrows, lanes), lambda i, *_: (i, 0))] * len(pieces)
            + [pl.BlockSpec((block,) + near.shape[1:], lambda i, *_: (first + i, 0, 0))],
            out_specs=pl.BlockSpec((block, rows, lanes), lambda i, *_: (i, 0, 0)),
            scratch_shapes=[pltpu.VMEM((block, rows, lanes), jnp.float32)],
        ),
        name="turn_right",
    )(place, *pieces, near)


def rotate_kernel(place, far_at, *refs, block, mrows, parts, stores, held, start, turned):
    pieces = refs[:parts]
    near = refs[parts]
    far_stores = refs[parts + 1 : parts + 1 + stores * block]
    out, gathered = refs[-2:]
    for k in range(block):
        values = collect(place, pieces, gathered, k, mrows)
        at = far_at[start + pl.program_id(0) * block + k]
        far = far_stores[k][0]
        for n in range(1, stores):
            far = jnp.where(at >= n * held, far_stores[n * block + k][0], far)
        right = values if turned else right_turn(values, near[k])
        for a, done in enumerate(left_turn(right, far)):
            out[k, a] = done


def rotate(pieces, near, far_stores, far_at, mrows, modes, start, place, before, turned=False):
    total, orbitals = near.shape[:2]
    block = 8
    first = start // block
    lanes = 2 * orbitals
    if mrows and len(pieces) == 1:
        kpoints = pieces[0].shape[1] // mrows
        piece_spec = pl.BlockSpec((pieces[0].shape[0], block * mrows, lanes), lambda i, *_: (0, i, 0))
    elif mrows:
        kpoints = pieces[0].shape[0] // mrows
        piece_spec = pl.BlockSpec((block * mrows, lanes), lambda i, *_: (i, 0))
    else:
        kpoints = pieces[0].shape[0]
        piece_spec = pl.BlockSpec((block, modes * orbitals, lanes), lambda i, *_: (i, 0, 0))
    prior = [] if before is None else [before]
    stores = len(far_stores)
    held = far_stores[0].shape[0]

    def far_spec(k):
        return pl.BlockSpec(
            (1, orbitals, lanes), lambda i, _, at: (lax.rem(at[start + i * block + k], held), 0, 0)
        )

    return pl.pallas_call(
        lambda *refs: rotate_kernel(
            *refs, block=block, mrows=mrows, parts=len(pieces), stores=stores, held=held, start=start,
            turned=turned
        ),
        out_shape=jax.ShapeDtypeStruct((total, modes, orbitals, lanes), jnp.float32),
        grid_spec=pltpu.PrefetchScalarGridSpec(
            num_scalar_prefetch=2,
            grid=(kpoints // block,),
            in_specs=[piece_spec] * len(pieces)
            + [pl.BlockSpec((block, orbitals, lanes), lambda i, *_: (first + i, 0, 0))]
            + [far_spec(k) for k in range(block)] * stores
            + [pl.BlockSpec(memory_space=pl.ANY)] * len(prior),
            out_specs=pl.BlockSpec((block, modes, orbitals, lanes), lambda i, *_: (first + i, 0, 0, 0)),
            scratch_shapes=[pltpu.VMEM((block, modes * orbitals, lanes), jnp.float32)],
        ),
        input_output_aliases={len(pieces) + stores * block + 3: 0} if prior else {},
        name="rotate",
    )(place, far_at, *pieces, near, *[x for x in far_stores for _ in range(block)], *prior)


def exchange(x):
    return lax.all_to_all(x, "ka", split_axis=0, concat_axis=0, tiled=True)


def send(blocks, patterns, devices):
    return [lax.ppermute(blocks[s], "ka", [(d, d ^ s) for d in range(devices)]) for s in patterns]


def picks(asked, value, capacity):
    position = jnp.cumsum(asked.astype(jnp.int32), -1) - 1
    chosen = asked[..., None, :] & (position[..., None, :] == jnp.arange(capacity)[:, None])
    return jnp.sum(jnp.where(chosen, value[..., None, :], 0), -1)


def rank(owner, devices):
    same = (owner[:, None] == jnp.arange(devices, dtype=jnp.int32)[None, :]).astype(jnp.int32)
    return jnp.sum((jnp.cumsum(same, 0) - same) * same, 1)


def placed_local(wannier_table, lattice, kpoint_grid, eigen_vectors, target_owner, target_slot):
    kpoints, orbitals = eigen_vectors.shape[:2]
    vectors, pairs = wannier_table.shape[1:]
    devices = lax.axis_size("ka")
    groups = lax.axis_size("grp")
    me = lax.axis_index("ka")
    mrows = pairs // orbitals
    modes = devices * mrows // orbitals
    lanes = 2 * orbitals
    capacity = 2 * kpoints // devices
    tiled = mrows % 8 == 0
    relayed = devices <= RELAYED and devices & (devices - 1) == 0 and tiled
    place = me.astype(jnp.int32).reshape(1)
    lattice_rows = jnp.concatenate([lattice, jnp.zeros((5, vectors), jnp.int32)], 0).astype(jnp.float32)

    own = jnp.concatenate(
        [kpoint_grid, target_owner[None], target_slot[None], jnp.zeros((3, kpoints), jnp.int32)], 0
    )
    everyone = lax.all_to_all(
        jnp.broadcast_to(own[None], (groups * devices, 8, kpoints)),
        ("grp", "ka"),
        split_axis=0,
        concat_axis=0,
        tiled=True,
    ).reshape(groups, devices, 8, kpoints)
    known = lax.dynamic_index_in_dim(everyone, lax.axis_index("grp"), 0, keepdims=False)
    far_rank = rank(target_owner, devices)

    def fill(rows, high, low, parts, ready=()):
        count = rows.shape[0] * rows.shape[1]
        return interpolate(rows.reshape(count, 8), lattice_rows, high, low, mrows, parts, ready)

    def plain():
        wanted = picks(known[:, 3] == me, known[:, 4], capacity)
        picked = eigen_vectors[wanted.reshape(-1)].reshape(devices, capacity * orbitals, lanes)
        fetched = exchange(picked).reshape(devices * capacity, orbitals, lanes)
        far_at = target_owner * capacity + far_rank
        high, low = prepare_table(wannier_table)
        [values] = fill(known.transpose(0, 2, 1).astype(jnp.float32), high, low, 1)
        pieces = exchange(values.reshape(devices, kpoints * mrows, lanes))
        if not tiled:
            pieces = pieces.reshape(devices, kpoints, mrows, lanes).transpose(1, 0, 2, 3)
            pieces = pieces.reshape(kpoints, devices * mrows, lanes)
        mrows_or_none = mrows if tiled else 0
        return rotate([pieces], eigen_vectors, [fetched], far_at, mrows_or_none, modes, 0, place, None)

    if not relayed:
        return plain()

    half = devices // 2
    side = me // half
    mirror = me ^ half
    in_half = [list(range(half)), list(range(half, devices))]
    near_known = lax.dynamic_slice_in_dim(known, side * half, half, 0)
    away_known = lax.dynamic_slice_in_dim(known, (1 - side) * half, half, 0)
    side_of = jnp.arange(devices, dtype=jnp.int32)[None, :, None] // half
    crossing = everyone[:, :, 3] // half != side_of
    owners = jnp.arange(devices, dtype=jnp.int32)
    counts = jnp.sum(
        (crossing & (everyone[:, :, 3] == owners[:, None, None, None])).astype(jnp.int32), (2, 3)
    )
    fits = jnp.max(counts) <= CROSSING * kpoints // 64

    def serve(held, wanted):
        picked = held[wanted.reshape(-1)].reshape(half, capacity * orbitals, lanes)
        got = lax.all_to_all(
            picked, "ka", split_axis=0, concat_axis=0, tiled=True, axis_index_groups=in_half
        )
        return got.reshape(half * capacity, orbitals, lanes)

    def asked_slots(block, owner):
        hit = (block[:, 3] == owner)[..., None] & (block[:, 4][..., None] == jnp.arange(kpoints))
        return jnp.any(hit, (0, 1))

    def relay(room):
        slots = jnp.arange(kpoints, dtype=jnp.int32)
        leaving = picks(asked_slots(away_known, me), slots, room)
        mirrored = lax.ppermute(
            eigen_vectors[leaving], "ka", [(d, d ^ half) for d in range(devices)]
        )
        from_near = serve(eigen_vectors, picks(near_known[:, 3] == me, near_known[:, 4], capacity))
        arrived = jnp.cumsum(asked_slots(near_known, mirror).astype(jnp.int32)) - 1
        at_slot = near_known[:, 4][..., None] == slots
        row_of = jnp.sum(jnp.where(at_slot, arrived, 0), -1)
        from_far = serve(mirrored, picks(near_known[:, 3] == mirror, row_of, capacity))

        at = target_owner % half * capacity + far_rank
        far_at = jnp.where(target_owner // half == side, at, at + half * capacity)

        high, low = prepare_table(wannier_table)
        grid_rows = known.transpose(0, 2, 1).astype(jnp.float32)
        turned_rows = grid_rows[me ^ owners]
        edges = [0, kpoints // 8 * 5, kpoints]
        sent = []
        for start, end in zip(edges, edges[1:]):
            last = False
            rows = (grid_rows if last else turned_rows)[:, start:end]
            values = fill(rows, high, low, 1 if last else devices, [far_at])
            if last:
                sent.append([exchange(values[0].reshape(devices, (end - start) * mrows, lanes))])
            else:
                crossed = send(values, range(half, half + LEADING), devices)
                crossed += send(values, range(half + LEADING, devices), devices)
                sent.append([values[0]] + send(values, range(1, half), devices) + crossed)

        out = None
        for c, pieces in enumerate(sent):
            early = c == 0
            if early:
                pieces = [turn_right(pieces, eigen_vectors, mrows, modes * orbitals, edges[c], place)]
            out = rotate(
                pieces,
                eigen_vectors,
                [from_near, from_far],
                far_at,
                0 if early else mrows,
                modes,
                edges[c],
                place,
                out,
                early,
            )
        return out

    if FORCE:
        return relay(FORCE)
    return lax.cond(fits, lambda: relay(CROSSING * kpoints // 64), plain)


def solution(mesh):
    placed = (
        P(None, "grp", "ka"),
        P(None, "grp"),
        P(None, ("grp", "ka")),
        P(("grp", "ka"), None, None),
        P(("grp", "ka")),
        P(("grp", "ka")),
    )
    return jax.shard_map(
        placed_local,
        mesh=mesh,
        in_specs=placed,
        out_specs=P(("grp", "ka"), None, None, None),
        check_vma=False,
    )
```

```python
import math

import jax
import jax.numpy as jnp
from jax import lax
from jax.experimental import pallas as pl
from jax.experimental.pallas import tpu as pltpu
from jax.sharding import PartitionSpec as P


KMESH = 64
RELAYED = 16
CROSSING = 48
FORCE = 0
BLOCK = 16
LEADING = 4

SIN_TERMS = [(-1.0) ** i * math.pi ** (2 * i + 1) / math.factorial(2 * i + 1) for i in range(7)]
COS_TERMS = [(-1.0) ** i * math.pi ** (2 * i) / math.factorial(2 * i) for i in range(8)]


def horner(terms, x):
    total = jnp.full_like(x, terms[-1])
    for term in terms[-2::-1]:
        total = total * x + term
    return total


def split(x):
    high = x.astype(jnp.bfloat16)
    return high, (x - high.astype(jnp.float32)).astype(jnp.bfloat16)


def dot(a, b):
    return jnp.dot(a, b, preferred_element_type=jnp.float32)


def dot3(a, b):
    return dot(a[0], b[0]) + dot(a[0], b[1]) + dot(a[1], b[0])


def table_kernel(table, high, low):
    lane = lax.broadcasted_iota(jnp.int32, (table.shape[1], 128), 1)
    first = lane < 64

    def put(half, at, value):
        a, b = split(value)
        high[half, :, at * 128 : (at + 1) * 128] = a
        low[half, :, at * 128 : (at + 1) * 128] = b

    for block in range(table.shape[2] // 128):
        cut = slice(block * 128, (block + 1) * 128)
        real, imag = table[0, :, cut], table[1, :, cut]
        real_turned, imag_turned = pltpu.roll(real, 64, 1), pltpu.roll(imag, 64, 1)
        put(0, 2 * block, jnp.where(first, real, imag_turned))
        put(0, 2 * block + 1, jnp.where(first, real_turned, imag))
        put(1, 2 * block, jnp.where(first, -imag, real_turned))
        put(1, 2 * block + 1, jnp.where(first, -imag_turned, real))


def prepare_table(table):
    vectors, pairs = table.shape[1:]
    rows = math.gcd(vectors, 128)
    high, low = pl.pallas_call(
        table_kernel,
        out_shape=[jax.ShapeDtypeStruct((2, vectors, 2 * pairs), jnp.bfloat16)] * 2,
        grid=(vectors // rows,),
        in_specs=[pl.BlockSpec((2, rows, pairs), lambda i: (0, i, 0))],
        out_specs=[pl.BlockSpec((2, rows, 2 * pairs), lambda i: (0, i, 0))] * 2,
        name="table",
    )(table)
    return high.reshape(2 * vectors, 2 * pairs), low.reshape(2 * vectors, 2 * pairs)


def interpolate_kernel(grid_rows, lattice, high, low, *refs, mrows, parts):
    outs = refs[-parts:]
    turns = dot(grid_rows[...].astype(jnp.bfloat16), lattice[...].astype(jnp.bfloat16)) * (1.0 / KMESH)
    part = turns - jnp.round(turns)
    square = part * part
    sine = horner(SIN_TERMS, square) * part
    cosine = horner(COS_TERMS, square)
    phase = jnp.concatenate([1.0 - 2.0 * sine * sine, 2.0 * sine * cosine], 1)
    result = dot3(split(phase), (high[...], low[...]))
    rows = result.shape[0]

    def store(out, first, count):
        for m in range(mrows):
            out[pl.ds(m, count, stride=mrows), :] = result[first : first + count, m * 128 : (m + 1) * 128]

    if parts == 1:
        store(outs[0], 0, rows)
        return
    each = outs[0].shape[0] // mrows
    per_step = rows // each
    for i in range(parts // per_step):

        @pl.when(pl.program_id(0) == i)
        def _():
            for j in range(per_step):
                store(outs[i * per_step + j], j * each, each)


def interpolate(grid_rows, lattice, high, low, mrows, parts, ready):
    rows = grid_rows.shape[0]
    unit = rows // parts if parts > 1 else 8
    step = max(n for n in range(unit, 257, unit) if rows % n == 0)
    whole = lambda a: pl.BlockSpec(a.shape, lambda i: (0, 0))
    if parts == 1:
        out_specs = [pl.BlockSpec((step * mrows, 128), lambda i: (i, 0))]
    else:
        out_specs = [pl.BlockSpec((unit * mrows, 128), lambda i: (0, 0))] * parts
    return pl.pallas_call(
        lambda *refs: interpolate_kernel(*refs, mrows=mrows, parts=parts),
        out_shape=[jax.ShapeDtypeStruct((rows // parts * mrows, 128), jnp.float32)] * parts,
        grid=(rows // step,),
        in_specs=[
            pl.BlockSpec((step, grid_rows.shape[1]), lambda i: (i, 0)),
            whole(lattice),
            whole(high),
            whole(low),
        ]
        + [pl.BlockSpec(memory_space=pl.ANY)] * len(ready),
        out_specs=out_specs,
        name="interpolate",
    )(grid_rows, lattice, high, low, *ready)


def right_turn(values, u):
    orbitals, lanes = u.shape
    first = lax.broadcasted_iota(jnp.int32, (orbitals, lanes), 1) < orbitals
    u_turned = pltpu.roll(u, orbitals, 1)
    u_full = jnp.concatenate([u, jnp.where(first, -u_turned, u_turned)], 0)
    return dot3(split(values), split(u_full))


def left_turn(right, far):
    orbitals, lanes = far.shape
    first = lax.broadcasted_iota(jnp.int32, right.shape, 1) < orbitals
    turned = pltpu.roll(right, orbitals, 1)
    turned = jnp.where(first, turned, -turned)
    v = far.T
    left = jnp.concatenate([v[:orbitals], v[orbitals:]], 1)
    modes = right.shape[0] // orbitals
    by_mode = lambda x: jnp.concatenate([x[a * orbitals : (a + 1) * orbitals] for a in range(modes)], 1)
    done = dot3(split(left), split(jnp.concatenate([by_mode(right), by_mode(turned)], 0)))
    return [done[:, a * lanes : (a + 1) * lanes] for a in range(modes)]


def collect(place, pieces, gathered, k, mrows):
    parts = len(pieces)
    if not mrows:
        return pieces[0][k]
    if parts == 1:
        return pieces[0][:, k * mrows : (k + 1) * mrows, :].reshape(gathered.shape[1:])
    for s in range(parts):
        at = pl.multiple_of((place[0] ^ s) * mrows, mrows)
        gathered[k, pl.ds(at, mrows), :] = pieces[s][k * mrows : (k + 1) * mrows, :]
    return gathered[k]


def right_kernel(place, *refs, block, mrows, parts):
    near, out, gathered = refs[parts:]
    for k in range(block):
        out[k] = right_turn(collect(place, refs[:parts], gathered, k, mrows), near[k])


def turn_right(pieces, near, mrows, rows, start, place):
    lanes = near.shape[2]
    kpoints = pieces[0].shape[0] // mrows
    block = math.gcd(BLOCK, kpoints, start)
    first = start // block
    return pl.pallas_call(
        lambda *refs: right_kernel(*refs, block=block, mrows=mrows, parts=len(pieces)),
        out_shape=jax.ShapeDtypeStruct((kpoints, rows, lanes), jnp.float32),
        grid_spec=pltpu.PrefetchScalarGridSpec(
            num_scalar_prefetch=1,
            grid=(kpoints // block,),
            in_specs=[pl.BlockSpec((block * mrows, lanes), lambda i, *_: (i, 0))] * len(pieces)
            + [pl.BlockSpec((block,) + near.shape[1:], lambda i, *_: (first + i, 0, 0))],
            out_specs=pl.BlockSpec((block, rows, lanes), lambda i, *_: (i, 0, 0)),
            scratch_shapes=[pltpu.VMEM((block, rows, lanes), jnp.float32)],
        ),
        name="turn_right",
    )(place, *pieces, near)


def rotate_kernel(place, far_at, *refs, block, mrows, parts, start, turned, stores):
    pieces = refs[:parts]
    held, rest = refs[parts : parts + stores], refs[parts + stores : -2]
    out, gathered = refs[-2:]
    room = held[0].shape[0]
    for k in range(block):
        at = far_at[start + pl.program_id(0) * block + k]
        v = held[0][jnp.minimum(at, room - 1)]
        if stores > 1:
            v = jnp.where(at >= room, held[1][jnp.maximum(at - room, 0)], v)
        right = collect(place, pieces, gathered, k, mrows)
        if not turned:
            right = right_turn(right, rest[0][k])
        for a, done in enumerate(left_turn(right, v)):
            out[k, a] = done


def rotate(pieces, near, held, far_at, mrows, modes, start, place, before):
    total = far_at.shape[0]
    orbitals, lanes = held[0].shape[1:]
    rows = modes * orbitals
    if mrows and len(pieces) == 1:
        kpoints = pieces[0].shape[1] // mrows
    elif mrows:
        kpoints = pieces[0].shape[0] // mrows
    else:
        kpoints = pieces[0].shape[0]
    block = math.gcd(BLOCK, kpoints, start)
    first = start // block
    if mrows and len(pieces) == 1:
        piece_spec = pl.BlockSpec((pieces[0].shape[0], block * mrows, lanes), lambda i, *_: (0, i, 0))
    elif mrows:
        piece_spec = pl.BlockSpec((block * mrows, lanes), lambda i, *_: (i, 0))
    else:
        piece_spec = pl.BlockSpec((block, rows, lanes), lambda i, *_: (i, 0, 0))
    vector_spec = pl.BlockSpec((block, orbitals, lanes), lambda i, *_: (first + i, 0, 0))
    turned = near is None
    operands = [*pieces, *held]
    specs = [piece_spec] * len(pieces) + [pl.BlockSpec(x.shape, lambda i, *_: (0, 0, 0)) for x in held]
    if not turned:
        operands.append(near)
        specs.append(vector_spec)
    if before is not None:
        operands.append(before)
        specs.append(pl.BlockSpec(memory_space=pl.ANY))
    return pl.pallas_call(
        lambda *refs: rotate_kernel(
            *refs,
            block=block,
            mrows=mrows,
            parts=len(pieces),
            start=start,
            turned=turned,
            stores=len(held),
        ),
        out_shape=jax.ShapeDtypeStruct((total, modes, orbitals, lanes), jnp.float32),
        grid_spec=pltpu.PrefetchScalarGridSpec(
            num_scalar_prefetch=2,
            grid=(kpoints // block,),
            in_specs=specs,
            out_specs=pl.BlockSpec((block, modes, orbitals, lanes), lambda i, *_: (first + i, 0, 0, 0)),
            scratch_shapes=[pltpu.VMEM((block, rows, lanes), jnp.float32)],
        ),
        input_output_aliases={} if before is None else {len(operands) + 1: 0},
        name="rotate",
    )(place, far_at, *operands)


def exchange(x):
    return lax.all_to_all(x, "ka", split_axis=0, concat_axis=0, tiled=True)


def send(blocks, patterns, devices):
    return [lax.ppermute(blocks[s], "ka", [(d, d ^ s) for d in range(devices)]) for s in patterns]


def picks(asked, value, capacity):
    position = jnp.cumsum(asked.astype(jnp.int32), -1) - 1
    chosen = asked[..., None, :] & (position[..., None, :] == jnp.arange(capacity)[:, None])
    return jnp.sum(jnp.where(chosen, value[..., None, :], 0), -1)


def rank(owner, devices):
    same = (owner[:, None] == jnp.arange(devices, dtype=jnp.int32)[None, :]).astype(jnp.int32)
    return jnp.sum((jnp.cumsum(same, 0) - same) * same, 1)


def placed_local(wannier_table, lattice, kpoint_grid, eigen_vectors, target_owner, target_slot):
    kpoints, orbitals = eigen_vectors.shape[:2]
    vectors, pairs = wannier_table.shape[1:]
    devices = lax.axis_size("ka")
    groups = lax.axis_size("grp")
    me = lax.axis_index("ka")
    mrows = pairs // orbitals
    modes = devices * mrows // orbitals
    lanes = 2 * orbitals
    capacity = 2 * kpoints // devices
    tiled = mrows % 8 == 0
    relayed = devices <= RELAYED and devices & (devices - 1) == 0 and tiled
    place = me.astype(jnp.int32).reshape(1)
    lattice_rows = jnp.concatenate([lattice, jnp.zeros((5, vectors), jnp.int32)], 0).astype(jnp.float32)

    own = jnp.concatenate(
        [kpoint_grid, target_owner[None], target_slot[None], jnp.zeros((3, kpoints), jnp.int32)], 0
    )
    everyone = lax.all_to_all(
        jnp.broadcast_to(own[None], (groups * devices, 8, kpoints)),
        ("grp", "ka"),
        split_axis=0,
        concat_axis=0,
        tiled=True,
    ).reshape(groups, devices, 8, kpoints)
    known = lax.dynamic_index_in_dim(everyone, lax.axis_index("grp"), 0, keepdims=False)
    far_rank = rank(target_owner, devices)

    def fill(rows, high, low, parts, ready=()):
        count = rows.shape[0] * rows.shape[1]
        return interpolate(rows.reshape(count, 8), lattice_rows, high, low, mrows, parts, ready)

    def plain():
        wanted = picks(known[:, 3] == me, known[:, 4], capacity)
        picked = eigen_vectors[wanted.reshape(-1)].reshape(devices, capacity * orbitals, lanes)
        fetched = exchange(picked).reshape(devices * capacity, orbitals, lanes)
        far_at = target_owner * capacity + far_rank
        high, low = prepare_table(wannier_table)
        [values] = fill(known.transpose(0, 2, 1).astype(jnp.float32), high, low, 1)
        pieces = exchange(values.reshape(devices, kpoints * mrows, lanes))
        if not tiled:
            pieces = pieces.reshape(devices, kpoints, mrows, lanes).transpose(1, 0, 2, 3)
            pieces = pieces.reshape(kpoints, devices * mrows, lanes)
        used = mrows if tiled else 0
        return rotate([pieces], eigen_vectors, [fetched], far_at, used, modes, 0, place, None)

    if not relayed:
        return plain()

    half = devices // 2
    side = me // half
    mirror = me ^ half
    in_half = [list(range(half)), list(range(half, devices))]
    near_known = lax.dynamic_slice_in_dim(known, side * half, half, 0)
    away_known = lax.dynamic_slice_in_dim(known, (1 - side) * half, half, 0)
    side_of = jnp.arange(devices, dtype=jnp.int32)[None, :, None] // half
    crossing = everyone[:, :, 3] // half != side_of
    owners = jnp.arange(devices, dtype=jnp.int32)
    counts = jnp.sum(
        (crossing & (everyone[:, :, 3] == owners[:, None, None, None])).astype(jnp.int32), (2, 3)
    )
    fits = jnp.max(counts) <= CROSSING * kpoints // 64

    def serve(held, wanted):
        picked = held[wanted.reshape(-1)].reshape(half, capacity * orbitals, lanes)
        got = lax.all_to_all(
            picked, "ka", split_axis=0, concat_axis=0, tiled=True, axis_index_groups=in_half
        )
        return got.reshape(half * capacity, orbitals, lanes)

    def asked_slots(block, owner):
        hit = (block[:, 3] == owner)[..., None] & (block[:, 4][..., None] == jnp.arange(kpoints))
        return jnp.any(hit, (0, 1))

    def relay(room):
        slots = jnp.arange(kpoints, dtype=jnp.int32)
        leaving = picks(asked_slots(away_known, me), slots, room)
        mirrored = lax.ppermute(
            eigen_vectors[leaving], "ka", [(d, d ^ half) for d in range(devices)]
        )
        from_near = serve(eigen_vectors, picks(near_known[:, 3] == me, near_known[:, 4], capacity))
        arrived = jnp.cumsum(asked_slots(near_known, mirror).astype(jnp.int32)) - 1
        at_slot = near_known[:, 4][..., None] == slots
        row_of = jnp.sum(jnp.where(at_slot, arrived, 0), -1)
        from_far = serve(mirrored, picks(near_known[:, 3] == mirror, row_of, capacity))

        at = target_owner % half * capacity + far_rank
        far_at = jnp.where(target_owner // half == side, at, at + half * capacity)

        high, low = prepare_table(wannier_table)
        grid_rows = known.transpose(0, 2, 1).astype(jnp.float32)
        turned_rows = grid_rows[me ^ owners]
        edges = [0, kpoints // 4 * 3, kpoints]
        sent = []
        for start, end in zip(edges, edges[1:]):
            last = False
            rows = (grid_rows if last else turned_rows)[:, start:end]
            values = fill(rows, high, low, 1 if last else devices, [far_at])
            if last:
                sent.append([exchange(values[0].reshape(devices, (end - start) * mrows, lanes))])
            else:
                crossed = send(values, range(half, half + LEADING), devices)
                crossed += send(values, range(half + LEADING, devices), devices)
                sent.append([values[0]] + send(values, range(1, half), devices) + crossed)

        out = None
        for c, pieces in enumerate(sent):
            early = c == 0
            if early:
                pieces = [turn_right(pieces, eigen_vectors, mrows, modes * orbitals, edges[c], place)]
            out = rotate(
                pieces,
                None if early else eigen_vectors,
                [from_near, from_far],
                far_at,
                0 if early else mrows,
                modes,
                edges[c],
                place,
                out,
            )
        return out

    if FORCE:
        return relay(FORCE)
    return lax.cond(fits, lambda: relay(CROSSING * kpoints // 64), plain)


def solution(mesh):
    placed = (
        P(None, "grp", "ka"),
        P(None, "grp"),
        P(None, ("grp", "ka")),
        P(("grp", "ka"), None, None),
        P(("grp", "ka")),
        P(("grp", "ka")),
    )
    return jax.shard_map(
        placed_local,
        mesh=mesh,
        in_specs=placed,
        out_specs=P(("grp", "ka"), None, None, None),
        check_vma=False,
    )
```
